32 devices in a mesh: rows: 8 (over z, y), cls: 4 (over x, core).
Axes of the slice: x: 2, y: 2, z: 4, core: 2. Of those that a mesh axis runs over, the one named last changes fastest.
Arguments:
- features: bfloat16 [6144, 2048], P('rows', 'cls'), may hold values from -32 to 32
- prototypes: bfloat16 [2048, 16384], P('rows', 'cls'), may hold values from -1 to 1
Outputs:
- grad_proto: float32 [2048, 16384], P('rows', 'cls')
The draws below stay inside these ranges and needn't reach their ends.
All inputs are finite; a program needn't handle non-finite values.
Results may differ from the reference program's by a relative error of at most 0.02.
Values may be sent and summed in bfloat16 or wider, within the bound.
A program may use at most 128 MiB of HBM per device.

```python
import jax
import jax.numpy as jnp
from jax import lax

D = 2048
K = 16384
B_DEV = 768
ITERS = 3
BATCH = 6144


def proto_matrix(key):
    proto_key = jax.random.fold_in(key, 101)
    base = jnp.clip(jax.random.normal(proto_key, (D, K), jnp.float32), -5.0, 5.0)
    return (base * D ** (-0.5)).astype(jnp.bfloat16).astype(jnp.float32)


def draw_prototypes(key, part):
    return proto_matrix(key).astype(jnp.bfloat16)


def draw_features(key, part):
    key_list = [jax.random.fold_in(key, 200 + index) for index in range(8)]
    blocks = BATCH // B_DEV
    block_width = D // blocks
    values = jnp.clip(jax.random.normal(key_list[0], (BATCH, D), jnp.float32), -4.0, 4.0)
    pairing = jax.random.permutation(key_list[3], blocks)
    row_block = jnp.arange(BATCH) // B_DEV
    col_block = jnp.arange(D) // block_width
    spike = jnp.where(col_block[None, :] == pairing[row_block][:, None], 3.0, 1.0)
    values = values * spike
    return jnp.clip(values, -32.0, 32.0).astype(jnp.bfloat16)


def setup_inputs(seed: int = 0) -> dict:
    key_of = jax.random.split(jax.random.key(seed), 3)
    features = draw_features(jax.random.fold_in(key_of[2], 71), 0)
    prototypes = draw_prototypes(jax.random.fold_in(key_of[2], 71), 0)
    return {"features": features, "prototypes": prototypes}


code_temp = 0.2
loss_temp = 0.3


def reference(features, prototypes):
    num_blocks = features.shape[0] // B_DEV
    classes = prototypes.shape[1]
    feat_blocks = features.reshape(num_blocks, B_DEV, features.shape[1])

    def first_pass(row_block):
        scores = jnp.dot(row_block, prototypes, preferred_element_type=jnp.float32)
        row_top = jnp.max(scores, axis=1, keepdims=True)
        exp_codes = jnp.exp((scores - row_top) / code_temp)
        soft_total = jnp.sum(jnp.exp((scores - row_top) / loss_temp), axis=1)
        return exp_codes, jnp.sum(exp_codes, axis=1), row_top[:, 0], soft_total

    exp_codes, sink_total, row_tops, soft_totals = lax.map(first_pass, feat_blocks)
    row_scale = 1.0 / sink_total
    col_scale = jnp.ones((classes,), jnp.float32)
    balance_ratio = jnp.float32(num_blocks * B_DEV) / jnp.float32(classes)
    for sweep in range(ITERS):
        col_mass = jnp.einsum("bi,bij->j", row_scale, exp_codes, precision=lax.Precision.HIGHEST) * col_scale
        col_scale = col_scale * balance_ratio / col_mass
        row_mass = jnp.einsum("bij,j->bi", exp_codes, col_scale, precision=lax.Precision.HIGHEST) * row_scale
        row_scale = row_scale / row_mass

    def grad_step(running, carried):
        row_block, exp_block, scale_rows, top_rows, soft_rows = carried
        scores = jnp.dot(row_block, prototypes, preferred_element_type=jnp.float32)
        probs_loss = jnp.exp((scores - top_rows[:, None]) / loss_temp) / soft_rows[:, None]
        codes = scale_rows[:, None] * exp_block * col_scale[None, :]
        slope = ((probs_loss - codes) / loss_temp).astype(jnp.bfloat16)
        partial_value = jnp.dot(row_block.T, slope, preferred_element_type=jnp.float32).astype(jnp.bfloat16)
        partial_value = lax.optimization_barrier(partial_value)
        return running + partial_value.astype(jnp.float32), None

    start_grad = jnp.zeros((features.shape[1], classes), jnp.float32)
    grad_proto, _ = lax.scan(grad_step, start_grad, (feat_blocks, exp_codes, row_scale, row_tops, soft_totals))
    return grad_proto
```

```python
import functools
import math

import jax
import jax.numpy as jnp
from jax import lax
from jax.experimental import pallas as pl
from jax.experimental.pallas import tpu as pltpu
from jax.sharding import PartitionSpec as P

ITERS = 3
code_temp = 0.2
loss_temp = 0.3
K2 = math.log2(math.e) / code_temp
K3 = math.log2(math.e) / loss_temp

MESH = pl.DeviceIdType.MESH
F32 = jnp.float32
BF16 = jnp.bfloat16
H = 4
LANES = 128
TILE = 64


def kernel(
    R, C, resident, feat, protos, out, *refs,
):
    if resident:
        G, fbuf = refs[0], None
        refs = refs[1:]
    else:
        G, fbuf = refs[:2]
        refs = refs[2:]
    (
        Pb, PT, S, E, SL, T, RY, CA, cs, kst, krc,
        st0, ra0, qs0, q0, res0, st1, ra1, qs1, q1, res1, wv, av, fv,
        lsem, up_s, dn_s, ln_r, ns, nr, ps, pr, zs, zr, ys, yr,
        xas, xar, xbs, xbr, xcs, xcr, ks, kr, gys, gyr, gzs, gzr,
    ) = refs
    Z = R // 2
    Zh = Z // 2
    RC = R // C
    Bl, dl = feat.shape
    hp = Bl // H
    dr, kc = protos.shape
    kl = kc // Z
    NQ, kq = T.shape[0], T.shape[3]
    NJ = Bl // LANES
    ratio = float(Bl * R) / float(kc * C)

    r = lax.axis_index("rows")
    c = lax.axis_index("cls")
    x, core = c // 2, c % 2
    z, y = r // 2, r % 2
    me = 2 * z + x
    x_near = (r, (1 - x) * 2 + core)
    y_near = (2 * z + 1 - y, c)
    partner = (r, x * 2 + 1 - core)

    def plane(t):
        return (2 * (t // 2) + y, 2 * (t % 2) + core)

    def flip(i):
        t, b = me, 1
        while b <= i:
            if (i // b) % 2:
                t = t + b * (1 - 2 * ((me // b) % 2))
            b *= 2
        return t

    barrier = pltpu.get_barrier_semaphore()
    for i in range(1, 2 * Z):
        pl.semaphore_signal(barrier, inc=1, device_id=plane(flip(i)), device_id_type=MESH)
    pl.semaphore_signal(barrier, inc=1, device_id=partner, device_id_type=MESH)
    pl.semaphore_signal(barrier, inc=1, device_id=y_near, device_id_type=MESH)

    def send(src, dst, send_sem, recv_sem, dest):
        return pltpu.make_async_remote_copy(
            src_ref=src, dst_ref=dst, send_sem=send_sem, recv_sem=recv_sem, device_id=dest, device_id_type=MESH
        )

    def piece(o, xx, co, h):
        return G.at[o, 2 * xx + co, pl.ds(h * hp, hp)]

    def origin(o, h, src):
        return piece(o, x, core, h) if src is None else src

    def line_up(o, h, src=None):
        return send(origin(o, h, src), piece(o, x, core, h), up_s.at[o, h], ln_r.at[o, h], (r + 2, c))

    def line_down(o, h, src=None):
        return send(origin(o, h, src), piece(o, x, core, h), dn_s.at[o, h], ln_r.at[o, h], (r - 2, c))

    def line_in(o, h):
        return send(piece(o, x, core, h), piece(o, x, core, h), up_s.at[o, h], ln_r.at[o, h], partner)

    def near(o, h, src=None):
        return send(origin(o, h, src), piece(o, x, core, h), ns.at[o, h], nr.at[o, h], x_near)

    def near_in(o, h):
        return send(piece(o, 1 - x, core, h), piece(o, 1 - x, core, h), ns.at[o, h], nr.at[o, h], x_near)

    def pair(side, o, h, src=None):
        xx = 1 - x if side else x
        dst = piece(o, xx, core, h)
        return send(dst if src is None else src, dst, ps.at[side, o, h], pr.at[side, o, h], partner)

    def pair_in(side, o, h):
        xx = 1 - x if side else x
        dst = piece(o, xx, 1 - core, h)
        return send(dst, dst, ps.at[side, o, h], pr.at[side, o, h], partner)

    def sides(k, fn):
        if k == 0:
            fn(z, 0)
            return

        @pl.when(z - k >= 0)
        def _():
            fn(z - k, -1)

        @pl.when(z + k < Z)
        def _():
            fn(z + k, 1)

    def spread(o, side, h, src=None):
        if side <= 0:

            @pl.when(z + 1 < Z)
            def _():
                line_up(o, h, src).start()

        if side >= 0:

            @pl.when(z >= 1)
            def _():
                line_down(o, h, src).start()

        near(o, h, src).start()
        pair(0, o, h, src).start()

    def my_cols(zd):
        return protos.at[:, pl.ds(pl.multiple_of(zd * kl, kl), kl)]

    def slab(zo, yo):
        ro = 2 * zo + yo
        return Pb.at[ro // RC, pl.ds(pl.multiple_of((ro % RC) * dr, dr), dr)]

    def proto_z(zd):
        return send(my_cols(zd), slab(z, y), zs.at[zd], zr.at[z], (2 * zd + y, c))

    def proto_z_in(zo):
        return send(slab(zo, y), slab(zo, y), zs.at[zo], zr.at[zo], partner)

    def proto_y(zo, src=None):
        return send(slab(zo, y) if src is None else src, slab(zo, y), ys.at[zo], yr.at[zo], y_near)

    def proto_y_in(zo):
        return send(slab(zo, 1 - y), slab(zo, 1 - y), ys.at[zo], yr.at[zo], y_near)

    own = pltpu.make_async_copy(feat, G.at[z, c], lsem.at[0])
    mine = pltpu.make_async_copy(my_cols(z), slab(z, y), lsem.at[1])
    own.start()
    mine.start()
    pl.semaphore_wait(barrier, 2 * Z + 1)

    for h in range(H):
        near(z, h, feat.at[pl.ds(h * hp, hp)]).start()
    for k in range(1, Z):
        sides(k, lambda o, side: proto_z(o).start())
    proto_y(z, my_cols(z)).start()
    for h in range(H):
        src = feat.at[pl.ds(h * hp, hp)]

        @pl.when(z + 1 < Z)
        def _():
            line_up(z, h, src).start()

        @pl.when(z >= 1)
        def _():
            line_down(z, h, src).start()

        pair(0, z, h, src).start()

    def do_line(k, h):
        def step(o, side):
            line_in(o, h).wait_recv()
            spread(o, side, h)

        sides(k, step)

    def do_near(k):
        def step(o, side):
            for h in range(H):
                near_in(o, h).wait_recv()
                pair(1, o, h).start()

        sides(k, step)

    def do_proto(k):
        def step(o, side):
            proto_z_in(o).wait_recv()
            proto_y(o).start()

        sides(k, step)

    def turn(n, _):
        i, t = n // (kl // 256), n % (kl // 256)
        cols = pl.ds(pl.multiple_of(t * 256, 256), 256)
        PT[i, cols] = Pb[i, :, cols].astype(F32).T.astype(BF16)
        return 0

    def prepare():
        for zo in range(Z):
            proto_y_in(zo).wait_recv()
        mine.wait()
        lax.fori_loop(0, C * (kl // 256), turn, 0)
        own.wait()

    def fetch(o, cc, slot):
        if resident:
            return G.at[o, cc]
        load = pltpu.make_async_copy(G.at[o, cc], fbuf.at[slot], lsem.at[2 + slot])
        load.start()
        load.wait()
        return fbuf.at[slot]

    def absorb(side, k):
        def step(o, _):
            xx = 1 - x if side else x
            if k == 0 and side == 0:
                for h in range(H):
                    pair_in(0, o, h).wait_recv()
            else:
                for h in range(H):
                    pair_in(side, o, h).wait_recv()
            fs = [fetch(o, 2 * xx + i, i) for i in (0, 1)]

            def tile(n, _):
                rows = pl.ds(pl.multiple_of(n * 256, 256), 256)
                part = sum(
                    lax.dot_general(PT[2 * xx + i], fs[i][rows], (((1,), (1,)), ((), ())), preferred_element_type=F32)
                    for i in (0, 1)
                )
                if side == 0:
                    S[o, :, rows] = part
                else:
                    S[o, :, rows] += part
                return 0

            lax.fori_loop(0, Bl // 256, tile, 0)

        sides(k, step)

    def lanes(j):
        return slice(j * LANES, (j + 1) * LANES)

    def fold(v):
        return jnp.sum(v.reshape(TILE // 8, 8, LANES), axis=0)

    def tile_rows(i):
        return pl.ds(pl.multiple_of(i * TILE, TILE), TILE)

    def first(k):
        def step(o, _):
            def peak(i, m):
                rows = tile_rows(i)
                return tuple(
                    jnp.maximum(m[j], jnp.max(S[o, rows, lanes(j)].reshape(TILE // 8, 8, LANES), axis=0)) for j in range(NJ)
                )

            low = jnp.full((8, LANES), -jnp.inf, F32)
            tops = lax.fori_loop(0, kl // TILE, peak, (low,) * NJ)
            tops = [jnp.max(t, axis=0, keepdims=True) for t in tops]

            def expo(i, acc):
                rows = tile_rows(i)
                res = []
                for j in range(NJ):
                    sh = S[o, rows, lanes(j)] - tops[j]
                    e2 = jnp.exp2(sh * K2)
                    e3 = jnp.exp2(sh * K3)
                    E[o, rows, lanes(j)] = e2
                    S[o, rows, lanes(j)] = e3
                    res.append((acc[j][0] + fold(e2), acc[j][1] + fold(e3)))
                return tuple(res)

            none = jnp.zeros((8, LANES), F32)
            sums = lax.fori_loop(0, kl // TILE, expo, ((none, none),) * NJ)
            for j in range(NJ):
                st0[o, 0, :, lanes(j)] = tops[j]
                st0[o, 1, :, lanes(j)] = jnp.sum(sums[j][0], axis=0, keepdims=True)
                st0[o, 2, :, lanes(j)] = jnp.sum(sums[j][1], axis=0, keepdims=True)

        sides(k, step)

    for h in range(H):
        do_line(1, h)
    do_near(0)
    for k in range(1, Z):
        do_proto(k)
    for h in range(H):
        do_line(2, h)
    do_near(1)
    prepare()
    todo = [(absorb, 0, 0), (absorb, 1, 0), (first, 0), (absorb, 0, 1), (absorb, 1, 1), (first, 1)]

    def run(job):
        job[0](*job[1:])

    for k in range(3, Z + 1):
        for h in range(H):
            if k < Z:
                do_line(k, h)
            if todo:
                run(todo.pop(0))
        do_near(k - 1)
        while todo:
            run(todo.pop(0))
        todo = [(absorb, 0, k - 1), (absorb, 1, k - 1), (first, k - 1)]
    while todo:
        run(todo.pop(0))

    def half(g):
        return pl.ds(g * Zh, Zh)

    def cross_a(e, st, ra):
        return send(st.at[half(1 - core)], ra, xas.at[e], xar.at[e], partner)

    def cross_b(e, i, qs, q):
        return send(qs, q.at[me], xbs.at[e, i], xbr.at[e, i], plane(flip(i)))

    def cross_c(e, res, g):
        return send(res.at[half(g)], res.at[half(g)], xcs.at[e], xcr.at[e], partner)

    def meet(e, st, ra, qs, q, res, join):
        cross_a(e, st, ra).wait_recv()
        qs[...] = join([st[half(core)], ra[...]])
        for i in range(2 * Z - 1, 0, -1):
            cross_b(e, i, qs, q).start()
        q[me] = qs[...]
        for i in range(2 * Z - 1, 0, -1):
            cross_b(e, i, qs, q).wait_recv()
        res[half(core)] = join([q[i] for i in range(2 * Z)])
        cross_c(e, res, core).start()

    def join_stats(parts):
        top = functools.reduce(jnp.maximum, [p[:, 0] for p in parts])
        s2 = sum(p[:, 1] * jnp.exp2((p[:, 0] - top) * K2) for p in parts)
        s3 = sum(p[:, 2] * jnp.exp2((p[:, 0] - top) * K3) for p in parts)
        return jnp.stack([top, s2, s3], axis=1)

    def join_sum(parts):
        return functools.reduce(jnp.add, parts)

    def col(g, more):
        def tile(i, _):
            rows = tile_rows(i)
            acc = CA[rows] if more else None
            for o in range(Zh):
                for j in range(NJ):
                    m = E[g * Zh + o, rows, lanes(j)] * wv[g * Zh + o, :, lanes(j)]
                    acc = m if acc is None else acc + m
            CA[rows] = acc
            return 0

        lax.fori_loop(0, kl // TILE, tile, 0)

    def row(sweep, g):
        for n in range(Zh):
            o = g * Zh + n

            def tile(i, acc):
                rows = tile_rows(i)
                scale = cs[rows]
                return tuple(acc[j] + fold(E[o, rows, lanes(j)] * scale) for j in range(NJ))

            sums = lax.fori_loop(0, kl // TILE, tile, (jnp.zeros((8, LANES), F32),) * NJ)
            for j in range(NJ):
                st1[sweep, o, 0, :, lanes(j)] = jnp.sum(sums[j], axis=0, keepdims=True) * fv[o, :, lanes(j)]

    def scales(g):
        for n in range(Zh):
            o = g * Zh + n
            down = st0[o, 0] - res0[o, 0]
            f2 = jnp.exp2(down * K2)
            fv[o] = f2
            wv[o] = f2 / res0[o, 1]
            av[o] = jnp.exp2(down * K3) / (res0[o, 2] * loss_temp)

    def rescale(sweep, g):
        for n in range(Zh):
            o = g * Zh + n
            wv[o] = fv[o] / res1[sweep, o, 0]

    cross_a(0, st0, ra0).start()
    meet(0, st0, ra0, qs0, q0, res0, join_stats)
    scales(core)

    for sweep in range(ITERS):
        col(core, False)
        if sweep == 0:
            cross_c(0, res0, 1 - core).wait_recv()
            scales(1 - core)
        else:
            cross_c(sweep, res1.at[sweep - 1], 1 - core).wait_recv()
            rescale(sweep - 1, 1 - core)
        col(1 - core, True)
        kst[sweep] = jnp.sum(CA[...].T, axis=0, keepdims=True)
        swap = send(kst.at[sweep], krc.at[sweep], ks.at[sweep], kr.at[sweep], y_near)
        swap.start()
        swap.wait_recv()
        scale = ratio / (kst[sweep] + krc[sweep])
        cs[...] = jnp.broadcast_to(scale, (LANES, kl)).T
        row(sweep, 1 - core)
        args = [a.at[sweep] for a in (st1, ra1, qs1, q1, res1)]
        cross_a(sweep + 1, args[0], args[1]).start()
        row(sweep, core)
        meet(sweep + 1, *args, join_sum)
        rescale(sweep, core)

    cross_c(ITERS, res1.at[ITERS - 1], 1 - core).wait_recv()
    rescale(ITERS - 1, 1 - core)

    def slope(q):
        def tile(n, _):
            o, i = n // (kq // TILE), n % (kq // TILE)
            rows = tile_rows(q * (kq // TILE) + i)
            scale = cs[rows] * (1.0 / loss_temp)
            for j in range(NJ):
                value = S[o, rows, lanes(j)] * av[o, :, lanes(j)] - E[o, rows, lanes(j)] * wv[o, :, lanes(j)] * scale
                SL[o, tile_rows(i), lanes(j)] = value.astype(BF16)
            return 0

        lax.fori_loop(0, Z * (kq // TILE), tile, 0)

    own_chunk = 2 * z // RC
    low = jnp.where(z < Zh, 1, 0)

    def chunk(t):
        if t == C - 1:
            return own_chunk
        down = C - 1 - t
        down = jnp.where(down > own_chunk, down, down - 1)
        up = jnp.where(t < own_chunk, t, t + 1)
        return low * down + (1 - low) * up

    def block_rows(ro):
        return pl.ds(pl.multiple_of((ro % RC) * dr, dr), dr)

    def grad_y(q, zo):
        ro = 2 * zo + 1 - y
        return send(T.at[q, ro // RC, block_rows(ro)], RY.at[q, zo], gys.at[q, zo], gyr.at[q, zo], y_near)

    def out_cols(zo, q):
        return out.at[:, pl.ds(pl.multiple_of(zo * kl + q * kq, kq), kq)]

    def grad_z(q, zo):
        return send(RY.at[q, zo], out_cols(z, q), gzs.at[q, zo], gzr.at[q, z], (2 * zo + y, c))

    def grad_z_in(q, zo):
        return send(RY.at[q, zo], out_cols(zo, q), gzs.at[q, zo], gzr.at[q, zo], partner)

    def keep(q):
        return pltpu.make_async_copy(RY.at[q, z], out_cols(z, q), gzs.at[q, z])

    def grads(q):
        for t in range(C):
            cc = chunk(t)
            total = None
            for o in range(Z):
                part = jnp.dot(SL[o], fetch(o, cc, o % 2)[...], preferred_element_type=F32)
                total = part if total is None else total + part
            T[q, cc] = total.T.astype(BF16)
            for n in range(RC // 2):
                grad_y(q, cc * (RC // 2) + n).start()

    def pass_on(q):
        for t in range(C):
            cc = chunk(t)
            for n in range(RC // 2):
                zo = cc * (RC // 2) + n
                ro = 2 * zo + y
                grad_y(q, zo).wait_recv()
                RY[q, zo] = (T[q, cc, block_rows(ro)].astype(F32) + RY[q, zo].astype(F32)).astype(BF16)

                @pl.when(zo != z)
                def _():
                    grad_z(q, zo).start()

                @pl.when(zo == z)
                def _():
                    keep(q).start()

    for q in range(NQ):
        slope(q)
        grads(q)
        if q >= 1:
            pass_on(q - 1)
    pass_on(NQ - 1)

    def drain(o, _):
        for h in range(H):

            @pl.when(jnp.logical_and(o <= z, z + 1 < Z))
            def _():
                line_up(o, h).wait_send()

            @pl.when(jnp.logical_and(o >= z, z >= 1))
            def _():
                line_down(o, h).wait_send()

            near(o, h).wait_send()
            pair(0, o, h).wait_send()
            pair(1, o, h).wait_send()
        proto_y(o).wait_send()

        @pl.when(o != z)
        def _():
            proto_z(o).wait_send()

        return 0

    lax.fori_loop(0, Z, drain, 0)

    cross_a(0, st0, ra0).wait_send()
    cross_c(0, res0, core).wait_send()
    for i in range(1, 2 * Z):
        cross_b(0, i, qs0, q0).wait_send()
    for sweep in range(ITERS):
        args = [a.at[sweep] for a in (st1, ra1, qs1, q1, res1)]
        send(kst.at[sweep], krc.at[sweep], ks.at[sweep], kr.at[sweep], y_near).wait_send()
        cross_a(sweep + 1, args[0], args[1]).wait_send()
        cross_c(sweep + 1, args[4], core).wait_send()
        for i in range(1, 2 * Z):
            cross_b(sweep + 1, i, args[2], args[3]).wait_send()

    def finish(n, _):
        q, zo = n // Z, n % Z
        grad_y(q, zo).wait_send()

        @pl.when(zo != z)
        def _():
            grad_z(q, zo).wait_send()
            grad_z_in(q, zo).wait_recv()

        @pl.when(zo == z)
        def _():
            keep(q).wait()

        return 0

    lax.fori_loop(0, NQ * Z, finish, 0)


def solution(mesh):
    R, C = mesh.shape["rows"], mesh.shape["cls"]
    assert C == 4 and R % 8 == 0

    def local(features, prototypes):
        Bl, dl = features.shape
        dr, kc = prototypes.shape
        Z, RC = R // 2, R // C
        Zh = Z // 2
        kl = kc // Z
        kq = max(LANES, kl // 4)
        NQ = kl // kq
        X = ITERS + 1
        dma = pltpu.SemaphoreType.DMA
        V = pltpu.VMEM
        resident = Z * C * Bl * dl * 2 <= 13 * 1024 * 1024
        gather = (V((Z, C, Bl, dl), BF16),) if resident else (V((2, Bl, dl), BF16),)
        outs = (jax.ShapeDtypeStruct((dr, kc), BF16),)
        if not resident:
            outs += (jax.ShapeDtypeStruct((Z, C, Bl, dl), BF16),)
        res = pl.pallas_call(
            functools.partial(kernel, R, C, resident),
            out_shape=outs,
            in_specs=[pl.BlockSpec(memory_space=pl.ANY)] * 2,
            out_specs=(pl.BlockSpec(memory_space=pl.ANY),) * len(outs),
            scratch_shapes=[
                *gather,
                V((C, dl, kl), BF16),
                V((C, kl, dl), BF16),
                V((Z, kl, Bl), F32),
                V((Z, kl, Bl), F32),
                V((Z, kq, Bl), BF16),
                V((NQ, C, dl, kq), BF16),
                V((NQ, Z, dr, kq), BF16),
                V((kl, LANES), F32),
                V((kl, LANES), F32),
                V((ITERS, 1, kl), F32),
                V((ITERS, 1, kl), F32),
                V((Z, 3, 1, Bl), F32),
                V((Zh, 3, 1, Bl), F32),
                V((Zh, 3, 1, Bl), F32),
                V((2 * Z, Zh, 3, 1, Bl), F32),
                V((Z, 3, 1, Bl), F32),
                V((ITERS, Z, 1, 1, Bl), F32),
                V((ITERS, Zh, 1, 1, Bl), F32),
                V((ITERS, Zh, 1, 1, Bl), F32),
                V((ITERS, 2 * Z, Zh, 1, 1, Bl), F32),
                V((ITERS, Z, 1, 1, Bl), F32),
                V((Z, 1, Bl), F32),
                V((Z, 1, Bl), F32),
                V((Z, 1, Bl), F32),
                dma((4,)),
                dma((Z, H)),
                dma((Z, H)),
                dma((Z, H)),
                dma((Z, H)),
                dma((Z, H)),
                dma((2, Z, H)),
                dma((2, Z, H)),
                dma((Z,)),
                dma((Z,)),
                dma((Z,)),
                dma((Z,)),
                dma((X,)),
                dma((X,)),
                dma((X, 2 * Z)),
                dma((X, 2 * Z)),
                dma((X,)),
                dma((X,)),
                dma((ITERS,)),
                dma((ITERS,)),
                dma((NQ, Z)),
                dma((NQ, Z)),
                dma((NQ, Z)),
                dma((NQ, Z)),
            ],
            compiler_params=pltpu.CompilerParams(
                collective_id=0, has_side_effects=True, vmem_limit_bytes=62 * 1024 * 1024
            ),
        )(features, prototypes)
        return res[0].astype(F32)

    return jax.shard_map(
        local,
        mesh=mesh,
        in_specs=(P("rows", "cls"), P("rows", "cls")),
        out_specs=P("rows", "cls"),
        check_vma=False,
    )
```

```python
import functools
import math

import jax
import jax.numpy as jnp
from jax import lax
from jax.experimental import pallas as pl
from jax.experimental.pallas import tpu as pltpu
from jax.sharding import PartitionSpec as P

ITERS = 3
code_temp = 0.2
loss_temp = 0.3
K2 = math.log2(math.e) / code_temp
K3 = math.log2(math.e) / loss_temp

MESH = pl.DeviceIdType.MESH
F32 = jnp.float32
BF16 = jnp.bfloat16
PARTS = 2
LANES = 128
TILE = 64
WIDE = 256
LAG = 3
AHEAD = 2
READY = 2


def kernel(
    R, C, resident, feat, protos, out, *refs,
):
    if resident:
        G, fbuf = refs[0], None
        refs = refs[1:]
    else:
        G, fbuf = refs[:2]
        refs = refs[2:]
    (
        Pb, PT, S, E, SL, T, RY, CA, cs, kst, krc,
        st0, ra0, qs0, q0, res0, st1, ra1, qs1, q1, res1, wv, av, fv,
        lsem, up_s, dn_s, ln_r, ns, nr, ps, pr, zs, zr, ys, yr,
        xas, xar, xbs, xbr, xcs, xcr, ks, kr, gys, gyr, gzs, gzr,
    ) = refs
    Z = R // 2
    Zh = Z // 2
    RC = R // C
    Bl, dl = feat.shape
    H = ln_r.shape[1]
    hp = Bl // H
    dr, kc = protos.shape
    kl = kc // Z
    NQ, kq = T.shape[0], T.shape[3]
    NJ = Bl // LANES
    ratio = float(Bl * R) / float(kc * C)

    r = lax.axis_index("rows")
    c = lax.axis_index("cls")
    x, core = c // 2, c % 2
    z, y = r // 2, r % 2
    me = 2 * z + x
    x_near = (r, (1 - x) * 2 + core)
    y_near = (2 * z + 1 - y, c)
    partner = (r, x * 2 + 1 - core)

    def plane(t):
        return (2 * (t // 2) + y, 2 * (t % 2) + core)

    def flip(i):
        t, b = me, 1
        while b <= i:
            if (i // b) % 2:
                t = t + b * (1 - 2 * ((me // b) % 2))
            b *= 2
        return t

    barrier = pltpu.get_barrier_semaphore()
    for i in range(1, 2 * Z):
        pl.semaphore_signal(barrier, inc=1, device_id=plane(flip(i)), device_id_type=MESH)
    pl.semaphore_signal(barrier, inc=1, device_id=partner, device_id_type=MESH)
    pl.semaphore_signal(barrier, inc=1, device_id=y_near, device_id_type=MESH)

    def send(src, dst, send_sem, recv_sem, dest):
        return pltpu.make_async_remote_copy(
            src_ref=src, dst_ref=dst, send_sem=send_sem, recv_sem=recv_sem, device_id=dest, device_id_type=MESH
        )

    def piece(o, xx, co, h):
        return G.at[o, 2 * xx + co, pl.ds(h * hp, hp)]

    def origin(o, h, src):
        return piece(o, x, core, h) if src is None else src

    def line_up(o, h, src=None):
        return send(origin(o, h, src), piece(o, x, core, h), up_s.at[o, h], ln_r.at[o, h], (r + 2, c))

    def line_down(o, h, src=None):
        return send(origin(o, h, src), piece(o, x, core, h), dn_s.at[o, h], ln_r.at[o, h], (r - 2, c))

    def line_in(o, h):
        return send(piece(o, x, core, h), piece(o, x, core, h), up_s.at[o, h], ln_r.at[o, h], partner)

    def near(o, h, src=None):
        return send(origin(o, h, src), piece(o, x, core, h), ns.at[o, h], nr.at[o, h], x_near)

    def near_in(o, h):
        return send(piece(o, 1 - x, core, h), piece(o, 1 - x, core, h), ns.at[o, h], nr.at[o, h], x_near)

    def pair(side, o, h, src=None):
        xx = 1 - x if side else x
        dst = piece(o, xx, core, h)
        return send(dst if src is None else src, dst, ps.at[side, o, h], pr.at[side, o, h], partner)

    def pair_in(side, o, h):
        xx = 1 - x if side else x
        dst = piece(o, xx, 1 - core, h)
        return send(dst, dst, ps.at[side, o, h], pr.at[side, o, h], partner)

    def sides(k, fn):
        if k == 0:
            fn(z, 0)
            return

        @pl.when(z - k >= 0)
        def _():
            fn(z - k, -1)

        @pl.when(z + k < Z)
        def _():
            fn(z + k, 1)

    def spread(o, side, h, src=None):
        if side <= 0:

            @pl.when(z + 1 < Z)
            def _():
                line_up(o, h, src).start()

        if side >= 0:

            @pl.when(z >= 1)
            def _():
                line_down(o, h, src).start()

        near(o, h, src).start()
        pair(0, o, h, src).start()

    NP = max(1, dr // 64)
    dp = dr // NP

    def my_cols(zd, p):
        return protos.at[pl.ds(p * dp, dp), pl.ds(pl.multiple_of(zd * kl, kl), kl)]

    def slab(zo, yo, p):
        ro = 2 * zo + yo
        return Pb.at[ro // RC, pl.ds(pl.multiple_of((ro % RC) * dr + p * dp, dp), dp)]

    def proto_z(zd, p):
        return send(my_cols(zd, p), slab(z, y, p), zs.at[zd, p], zr.at[z, p], (2 * zd + y, c))

    def proto_z_in(zo, p):
        return send(slab(zo, y, p), slab(zo, y, p), zs.at[zo, p], zr.at[zo, p], partner)

    def proto_y(zo, p, src=None):
        return send(slab(zo, y, p) if src is None else src, slab(zo, y, p), ys.at[zo, p], yr.at[zo, p], y_near)

    def proto_y_in(zo, p):
        return send(slab(zo, 1 - y, p), slab(zo, 1 - y, p), ys.at[zo, p], yr.at[zo, p], y_near)

    own = pltpu.make_async_copy(feat, G.at[z, c], lsem.at[0])
    mine = pltpu.make_async_copy(
        protos.at[:, pl.ds(pl.multiple_of(z * kl, kl), kl)],
        Pb.at[r // RC, pl.ds(pl.multiple_of((r % RC) * dr, dr), dr)],
        lsem.at[1],
    )
    own.start()
    mine.start()
    pl.semaphore_wait(barrier, 2 * Z + 1)

    for h in range(H):
        src = feat.at[pl.ds(h * hp, hp)]
        near(z, h, src).start()
        pair(0, z, h, src).start()
    order = [("line", h) for h in range(AHEAD)]
    for p in range(NP):
        order += [("proto", p)] + ([("line", AHEAD + p)] if AHEAD + p < H else [])
    order += [("line", h) for h in range(AHEAD + NP, H)]

    for kind, n in order:
        if kind == "proto":
            for k in range(Z - 1, 0, -1):
                sides(k, lambda o, side: proto_z(o, n).start())
            proto_y(z, n, my_cols(z, n)).start()
        else:
            src = feat.at[pl.ds(n * hp, hp)]

            @pl.when(z + 1 < Z)
            def _():
                line_up(z, n, src).start()

            @pl.when(z >= 1)
            def _():
                line_down(z, n, src).start()

    def do_line(k, h):
        def step(o, side):
            line_in(o, h).wait_recv()
            spread(o, side, h)

        sides(k, step)

    def do_near(k, h):
        def step(o, side):
            near_in(o, h).wait_recv()
            pair(1, o, h).start()

        sides(k, step)

    def do_proto(k, p):
        def step(o, side):
            proto_z_in(o, p).wait_recv()
            proto_y(o, p).start()

        sides(k, step)

    def turn(n, _):
        i, t = n // (kl // 256), n % (kl // 256)
        cols = pl.ds(pl.multiple_of(t * 256, 256), 256)
        PT[i, cols] = Pb[i, :, cols].astype(F32).T.astype(BF16)
        return 0

    def prepare():
        for p in range(NP):
            for zo in range(Z):
                proto_y_in(zo, p).wait_recv()
        mine.wait()
        lax.fori_loop(0, C * (kl // 256), turn, 0)
        own.wait()

    def fetch(o, cc, slot):
        if resident:
            return G.at[o, cc]
        load = pltpu.make_async_copy(G.at[o, cc], fbuf.at[slot], lsem.at[2 + slot])
        load.start()
        load.wait()
        return fbuf.at[slot]

    def lanes(j):
        return slice(j * LANES, (j + 1) * LANES)

    def fold(v):
        return jnp.sum(v.reshape(v.shape[0] // 8, 8, LANES), axis=0)

    def tile_rows(i):
        return pl.ds(pl.multiple_of(i * TILE, TILE), TILE)

    HT = H * 256 // Bl

    def unit(k, n):
        def step(o):
            for h in range(n * HT, (n + 1) * HT):
                for side in (0, 1):
                    pair_in(side, o, h).wait_recv()
            rows = slice(n * 256, (n + 1) * 256)
            total = None
            for i in range(C):
                part = lax.dot_general(PT[i], fetch(o, i, i % 2)[rows], (((1,), (1,)), ((), ())), preferred_element_type=F32)
                total = part if total is None else total + part
            S[o, :, rows] = total
            js = (2 * n, 2 * n + 1)

            def peak(i, m):
                part = pl.ds(pl.multiple_of(i * WIDE, WIDE), WIDE)
                return tuple(jnp.maximum(m[b], jnp.max(S[o, part, lanes(j)].reshape(WIDE // 8, 8, LANES), axis=0)) for b, j in enumerate(js))

            floor = jnp.full((8, LANES), -jnp.inf, F32)
            tops = lax.fori_loop(0, kl // WIDE, peak, (floor,) * 2)
            tops = [jnp.max(t, axis=0, keepdims=True) for t in tops]

            def expo(i, acc):
                part = pl.ds(pl.multiple_of(i * WIDE, WIDE), WIDE)
                res = []
                for b, j in enumerate(js):
                    sh = S[o, part, lanes(j)] - tops[b]
                    e2 = jnp.exp2(sh * K2)
                    e3 = jnp.exp2(sh * K3)
                    E[o, part, lanes(j)] = e2
                    S[o, part, lanes(j)] = e3
                    res.append((acc[b][0] + fold(e2), acc[b][1] + fold(e3)))
                return tuple(res)

            none = jnp.zeros((8, LANES), F32)
            sums = lax.fori_loop(0, kl // WIDE, expo, ((none, none),) * 2)
            for b, j in enumerate(js):
                st0[o, 0, :, lanes(j)] = tops[b]
                st0[o, 1, :, lanes(j)] = jnp.sum(sums[b][0], axis=0, keepdims=True)
                st0[o, 2, :, lanes(j)] = jnp.sum(sums[b][1], axis=0, keepdims=True)

        if k == 0:
            step(z)
            return

        def side(i, _):
            o = z + k * (2 * i - 1)

            @pl.when(jnp.logical_and(o >= 0, o < Z))
            def _():
                step(o)

            return 0

        lax.fori_loop(0, 2, side, 0)

    todo = [(0, n) for n in range(Bl // 256)]
    steps = [("proto", n) if kind == "proto" else ("line", 1, n) for kind, n in order]
    steps += [("line", k, h) for k in range(2, Z) for h in range(H)]
    steps += [("none",)] * LAG
    lines, left = 0, NP
    wait_ready = READY
    for step in steps:
        if step[0] == "proto":
            for k in range(1, Z):
                do_proto(k, step[1])
            left -= 1
            if left == NP // 2:
                for h in range(H):
                    do_near(0, h)
            continue
        if step[0] == "line":
            do_line(step[1], step[2])
        lines += 1
        if lines > LAG:
            k, h = 1 + (lines - LAG - 1) // H, (lines - LAG - 1) % H
            do_near(k, h)
            if (h + 1) % HT == 0:
                todo.append((k, h // HT))
        if left == 0:
            wait_ready -= 1
            if wait_ready == 0:
                prepare()
            elif wait_ready < 0 and todo:
                unit(*todo.pop(0))
    while todo:
        unit(*todo.pop(0))

    def half(g):
        return pl.ds(g * Zh, Zh)

    def cross_a(e, st, ra):
        return send(st.at[half(1 - core)], ra, xas.at[e], xar.at[e], partner)

    def cross_b(e, i, qs, q):
        return send(qs, q.at[me], xbs.at[e, i], xbr.at[e, i], plane(flip(i)))

    def cross_c(e, res, g):
        return send(res.at[half(g)], res.at[half(g)], xcs.at[e], xcr.at[e], partner)

    def meet(e, st, ra, qs, q, res, join):
        cross_a(e, st, ra).wait_recv()
        qs[...] = join([st[half(core)], ra[...]])
        for i in range(2 * Z - 1, 0, -1):
            cross_b(e, i, qs, q).start()
        q[me] = qs[...]
        for i in range(2 * Z - 1, 0, -1):
            cross_b(e, i, qs, q).wait_recv()
        res[half(core)] = join([q[i] for i in range(2 * Z)])
        cross_c(e, res, core).start()

    def join_stats(parts):
        top = functools.reduce(jnp.maximum, [p[:, 0] for p in parts])
        s2 = sum(p[:, 1] * jnp.exp2((p[:, 0] - top) * K2) for p in parts)
        s3 = sum(p[:, 2] * jnp.exp2((p[:, 0] - top) * K3) for p in parts)
        return jnp.stack([top, s2, s3], axis=1)

    def join_sum(parts):
        return functools.reduce(jnp.add, parts)

    def col(g, more):
        def tile(i, _):
            rows = tile_rows(i)
            acc = CA[rows] if more else None
            for o in range(Zh):
                for j in range(NJ):
                    m = E[g * Zh + o, rows, lanes(j)] * wv[g * Zh + o, :, lanes(j)]
                    acc = m if acc is None else acc + m
            CA[rows] = acc
            return 0

        lax.fori_loop(0, kl // TILE, tile, 0)

    def row(sweep, g):
        for n in range(Zh):
            o = g * Zh + n

            def tile(i, acc):
                rows = tile_rows(i)
                scale = cs[rows]
                return tuple(acc[j] + fold(E[o, rows, lanes(j)] * scale) for j in range(NJ))

            sums = lax.fori_loop(0, kl // TILE, tile, (jnp.zeros((8, LANES), F32),) * NJ)
            for j in range(NJ):
                st1[sweep, o, 0, :, lanes(j)] = jnp.sum(sums[j], axis=0, keepdims=True) * fv[o, :, lanes(j)]

    def scales(g):
        for n in range(Zh):
            o = g * Zh + n
            down = st0[o, 0] - res0[o, 0]
            f2 = jnp.exp2(down * K2)
            fv[o] = f2
            wv[o] = f2 / res0[o, 1]
            av[o] = jnp.exp2(down * K3) / (res0[o, 2] * loss_temp)

    def rescale(sweep, g):
        for n in range(Zh):
            o = g * Zh + n
            wv[o] = fv[o] / res1[sweep, o, 0]

    cross_a(0, st0, ra0).start()
    meet(0, st0, ra0, qs0, q0, res0, join_stats)
    scales(core)

    for sweep in range(ITERS):
        col(core, False)
        if sweep == 0:
            cross_c(0, res0, 1 - core).wait_recv()
            scales(1 - core)
        else:
            cross_c(sweep, res1.at[sweep - 1], 1 - core).wait_recv()
            rescale(sweep - 1, 1 - core)
        col(1 - core, True)
        kst[sweep] = jnp.sum(CA[...].T, axis=0, keepdims=True)
        swap = send(kst.at[sweep], krc.at[sweep], ks.at[sweep], kr.at[sweep], y_near)
        swap.start()
        swap.wait_recv()
        scale = ratio / (kst[sweep] + krc[sweep])
        cs[...] = jnp.broadcast_to(scale, (LANES, kl)).T
        row(sweep, 1 - core)
        args = [a.at[sweep] for a in (st1, ra1, qs1, q1, res1)]
        cross_a(sweep + 1, args[0], args[1]).start()
        row(sweep, core)
        meet(sweep + 1, *args, join_sum)
        rescale(sweep, core)

    cross_c(ITERS, res1.at[ITERS - 1], 1 - core).wait_recv()
    rescale(ITERS - 1, 1 - core)

    def slope(q):
        def tile(n, _):
            o, i = n // (kq // TILE), n % (kq // TILE)
            rows = tile_rows(q * (kq // TILE) + i)
            scale = cs[rows] * (1.0 / loss_temp)
            for j in range(NJ):
                value = S[o, rows, lanes(j)] * av[o, :, lanes(j)] - E[o, rows, lanes(j)] * wv[o, :, lanes(j)] * scale
                SL[o, tile_rows(i), lanes(j)] = value.astype(BF16)
            return 0

        lax.fori_loop(0, Z * (kq // TILE), tile, 0)

    own_chunk = 2 * z // RC
    low = jnp.where(z < Zh, 1, 0)

    def chunk(t):
        if t == C - 1:
            return own_chunk
        down = C - 1 - t
        down = jnp.where(down > own_chunk, down, down - 1)
        up = jnp.where(t < own_chunk, t, t + 1)
        return low * down + (1 - low) * up

    ds = dr // PARTS

    def block_rows(ro, s):
        return pl.ds(pl.multiple_of((ro % RC) * dr + s * ds, ds), ds)

    def piece_of(q, zo, s):
        return RY.at[q, zo, pl.ds(s * ds, ds)]

    def grad_y(q, zo, s):
        ro = 2 * zo + 1 - y
        return send(T.at[q, ro // RC, block_rows(ro, s)], piece_of(q, zo, s), gys.at[q, zo, s], gyr.at[q, zo, s], y_near)

    def out_part(zo, q, s):
        return out.at[pl.ds(s * ds, ds), pl.ds(pl.multiple_of(zo * kl + q * kq, kq), kq)]

    def grad_z(q, zo, s):
        return send(piece_of(q, zo, s), out_part(z, q, s), gzs.at[q, zo, s], gzr.at[q, z, s], (2 * zo + y, c))

    def grad_z_in(q, zo, s):
        return send(piece_of(q, zo, s), out_part(zo, q, s), gzs.at[q, zo, s], gzr.at[q, zo, s], partner)

    def keep(q, s):
        return pltpu.make_async_copy(piece_of(q, z, s), out_part(z, q, s), gzs.at[q, z, s])

    def grads(q, t):
        cc = chunk(t)
        total = None
        for o in range(Z):
            part = jnp.dot(SL[o], fetch(o, cc, o % 2)[...], preferred_element_type=F32)
            total = part if total is None else total + part
        T[q, cc] = total.T.astype(BF16)
        for n in range(RC // 2):
            for s in range(PARTS):
                grad_y(q, cc * (RC // 2) + n, s).start()

    def pass_on(q, t):
        cc = chunk(t)
        for n in range(RC // 2):
            zo = cc * (RC // 2) + n
            ro = 2 * zo + y
            for s in range(PARTS):
                grad_y(q, zo, s).wait_recv()
                part = pl.ds(s * ds, ds)
                RY[q, zo, part] = (T[q, cc, block_rows(ro, s)].astype(F32) + RY[q, zo, part].astype(F32)).astype(BF16)

                @pl.when(zo != z)
                def _():
                    grad_z(q, zo, s).start()

                @pl.when(zo == z)
                def _():
                    keep(q, s).start()

    for q in range(NQ):
        slope(q)
        for t in range(C):
            grads(q, t)
            if q >= 1:
                pass_on(q - 1, t)
    for t in range(C):
        pass_on(NQ - 1, t)

    def drain(o, _):
        for h in range(H):

            @pl.when(jnp.logical_and(o <= z, z + 1 < Z))
            def _():
                line_up(o, h).wait_send()

            @pl.when(jnp.logical_and(o >= z, z >= 1))
            def _():
                line_down(o, h).wait_send()

            near(o, h).wait_send()
            pair(0, o, h).wait_send()
            pair(1, o, h).wait_send()
        for p in range(NP):
            proto_y(o, p).wait_send()

            @pl.when(o != z)
            def _():
                proto_z(o, p).wait_send()

        return 0

    lax.fori_loop(0, Z, drain, 0)

    cross_a(0, st0, ra0).wait_send()
    cross_c(0, res0, core).wait_send()
    for i in range(1, 2 * Z):
        cross_b(0, i, qs0, q0).wait_send()
    for sweep in range(ITERS):
        args = [a.at[sweep] for a in (st1, ra1, qs1, q1, res1)]
        send(kst.at[sweep], krc.at[sweep], ks.at[sweep], kr.at[sweep], y_near).wait_send()
        cross_a(sweep + 1, args[0], args[1]).wait_send()
        cross_c(sweep + 1, args[4], core).wait_send()
        for i in range(1, 2 * Z):
            cross_b(sweep + 1, i, args[2], args[3]).wait_send()

    def finish(n, _):
        q, zo = n // Z, n % Z
        for s in range(PARTS):
            grad_y(q, zo, s).wait_send()

            @pl.when(zo != z)
            def _():
                grad_z(q, zo, s).wait_send()
                grad_z_in(q, zo, s).wait_recv()

            @pl.when(zo == z)
            def _():
                keep(q, s).wait()

        return 0

    lax.fori_loop(0, NQ * Z, finish, 0)


def solution(mesh):
    R, C = mesh.shape["rows"], mesh.shape["cls"]
    assert C == 4 and R % 8 == 0

    def local(features, prototypes):
        Bl, dl = features.shape
        dr, kc = prototypes.shape
        Z, RC = R // 2, R // C
        Zh = Z // 2
        kl = kc // Z
        kq = max(LANES, kl // 4)
        NQ = kl // kq
        NP = max(1, dr // 64)
        H = Bl // (128 if Z <= 4 else 256)
        X = ITERS + 1
        dma = pltpu.SemaphoreType.DMA
        V = pltpu.VMEM
        resident = Z * C * Bl * dl * 2 <= 13 * 1024 * 1024
        gather = (V((Z, C, Bl, dl), BF16),) if resident else (V((2, Bl, dl), BF16),)
        outs = (jax.ShapeDtypeStruct((dr, kc), BF16),)
        if not resident:
            outs += (jax.ShapeDtypeStruct((Z, C, Bl, dl), BF16),)
        res = pl.pallas_call(
            functools.partial(kernel, R, C, resident),
            out_shape=outs,
            in_specs=[pl.BlockSpec(memory_space=pl.ANY)] * 2,
            out_specs=(pl.BlockSpec(memory_space=pl.ANY),) * len(outs),
            scratch_shapes=[
                *gather,
                V((C, dl, kl), BF16),
                V((C, kl, dl), BF16),
                V((Z, kl, Bl), F32),
                V((Z, kl, Bl), F32),
                V((Z, kq, Bl), BF16),
                V((NQ, C, dl, kq), BF16),
                V((NQ, Z, dr, kq), BF16),
                V((kl, LANES), F32),
                V((kl, LANES), F32),
                V((ITERS, 1, kl), F32),
                V((ITERS, 1, kl), F32),
                V((Z, 3, 1, Bl), F32),
                V((Zh, 3, 1, Bl), F32),
                V((Zh, 3, 1, Bl), F32),
                V((2 * Z, Zh, 3, 1, Bl), F32),
                V((Z, 3, 1, Bl), F32),
                V((ITERS, Z, 1, 1, Bl), F32),
                V((ITERS, Zh, 1, 1, Bl), F32),
                V((ITERS, Zh, 1, 1, Bl), F32),
                V((ITERS, 2 * Z, Zh, 1, 1, Bl), F32),
                V((ITERS, Z, 1, 1, Bl), F32),
                V((Z, 1, Bl), F32),
                V((Z, 1, Bl), F32),
                V((Z, 1, Bl), F32),
                dma((4,)),
                dma((Z, H)),
                dma((Z, H)),
                dma((Z, H)),
                dma((Z, H)),
                dma((Z, H)),
                dma((2, Z, H)),
                dma((2, Z, H)),
                dma((Z, NP)),
                dma((Z, NP)),
                dma((Z, NP)),
                dma((Z, NP)),
                dma((X,)),
                dma((X,)),
                dma((X, 2 * Z)),
                dma((X, 2 * Z)),
                dma((X,)),
                dma((X,)),
                dma((ITERS,)),
                dma((ITERS,)),
                dma((NQ, Z, PARTS)),
                dma((NQ, Z, PARTS)),
                dma((NQ, Z, PARTS)),
                dma((NQ, Z, PARTS)),
            ],
            compiler_params=pltpu.CompilerParams(
                collective_id=0, has_side_effects=True, vmem_limit_bytes=62 * 1024 * 1024
            ),
        )(features, prototypes)
        return res[0].astype(F32)

    return jax.shard_map(
        local,
        mesh=mesh,
        in_specs=(P("rows", "cls"), P("rows", "cls")),
        out_specs=P("rows", "cls"),
        check_vma=False,
    )
```

```python
import functools
import math

import jax
import jax.numpy as jnp
from jax import lax
from jax.experimental import pallas as pl
from jax.experimental.pallas import tpu as pltpu
from jax.sharding import PartitionSpec as P

ITERS = 3
code_temp = 0.2
loss_temp = 0.3
K2 = math.log2(math.e) / code_temp
K3 = math.log2(math.e) / loss_temp

MESH = pl.DeviceIdType.MESH
F32 = jnp.float32
BF16 = jnp.bfloat16
PARTS = 2
LANES = 128
TILE = 256
WIDE = 256
LAG = 3
AHEAD = 3
READY = 2


def kernel(
    R, C, resident, feat, protos, out, *refs,
):
    if resident:
        G, fbuf = refs[0], None
        refs = refs[1:]
    else:
        G, fbuf = refs[:2]
        refs = refs[2:]
    (
        Pb, PT, S, E, SL, T, RY, CA, cs, kst, krc,
        st0, ra0, qs0, q0, res0, st1, ra1, qs1, q1, res1, wv, av, fv,
        lsem, up_s, dn_s, ln_r, ns, nr, ps, pr, zs, zr, ys, yr,
        xas, xar, xbs, xbr, xcs, xcr, ks, kr, gys, gyr, gzs, gzr,
    ) = refs
    Z = R // 2
    Zh = Z // 2
    RC = R // C
    Bl, dl = feat.shape
    H = ln_r.shape[1]
    hp = Bl // H
    dr, kc = protos.shape
    kl = kc // Z
    NQ, kq = T.shape[0], T.shape[3]
    NJ = Bl // LANES
    ratio = float(Bl * R) / float(kc * C)

    r = lax.axis_index("rows")
    c = lax.axis_index("cls")
    x, core = c // 2, c % 2
    z, y = r // 2, r % 2
    me = 2 * z + x
    x_near = (r, (1 - x) * 2 + core)
    y_near = (2 * z + 1 - y, c)
    partner = (r, x * 2 + 1 - core)

    def plane(t):
        return (2 * (t // 2) + y, 2 * (t % 2) + core)

    def flip(i):
        t, b = me, 1
        while b <= i:
            if (i // b) % 2:
                t = t + b * (1 - 2 * ((me // b) % 2))
            b *= 2
        return t

    barrier = pltpu.get_barrier_semaphore()
    for i in range(1, 2 * Z):
        pl.semaphore_signal(barrier, inc=1, device_id=plane(flip(i)), device_id_type=MESH)
    pl.semaphore_signal(barrier, inc=1, device_id=partner, device_id_type=MESH)
    pl.semaphore_signal(barrier, inc=1, device_id=y_near, device_id_type=MESH)

    def send(src, dst, send_sem, recv_sem, dest):
        return pltpu.make_async_remote_copy(
            src_ref=src, dst_ref=dst, send_sem=send_sem, recv_sem=recv_sem, device_id=dest, device_id_type=MESH
        )

    def piece(o, xx, co, h):
        return G.at[o, 2 * xx + co, pl.ds(h * hp, hp)]

    def origin(o, h, src):
        return piece(o, x, core, h) if src is None else src

    def line_up(o, h, src=None):
        return send(origin(o, h, src), piece(o, x, core, h), up_s.at[o, h], ln_r.at[o, h], (r + 2, c))

    def line_down(o, h, src=None):
        return send(origin(o, h, src), piece(o, x, core, h), dn_s.at[o, h], ln_r.at[o, h], (r - 2, c))

    def line_in(o, h):
        return send(piece(o, x, core, h), piece(o, x, core, h), up_s.at[o, h], ln_r.at[o, h], partner)

    def near(o, h, src=None):
        return send(origin(o, h, src), piece(o, x, core, h), ns.at[o, h], nr.at[o, h], x_near)

    def near_in(o, h):
        return send(piece(o, 1 - x, core, h), piece(o, 1 - x, core, h), ns.at[o, h], nr.at[o, h], x_near)

    def pair(side, o, h, src=None):
        xx = 1 - x if side else x
        dst = piece(o, xx, core, h)
        return send(dst if src is None else src, dst, ps.at[side, o, h], pr.at[side, o, h], partner)

    def pair_in(side, o, h):
        xx = 1 - x if side else x
        dst = piece(o, xx, 1 - core, h)
        return send(dst, dst, ps.at[side, o, h], pr.at[side, o, h], partner)

    def sides(k, fn):
        if isinstance(k, int) and k == 0:
            fn(z, 0)
            return

        @pl.when(z - k >= 0)
        def _():
            fn(z - k, -1)

        @pl.when(z + k < Z)
        def _():
            fn(z + k, 1)

    def spread(o, side, h, src=None):
        if side <= 0:

            @pl.when(z + 1 < Z)
            def _():
                line_up(o, h, src).start()

        if side >= 0:

            @pl.when(z >= 1)
            def _():
                line_down(o, h, src).start()

        near(o, h, src).start()
        pair(0, o, h, src).start()

    NP = max(1, dr // 64)
    dp = dr // NP

    def my_cols(zd, p):
        return protos.at[pl.ds(p * dp, dp), pl.ds(pl.multiple_of(zd * kl, kl), kl)]

    def slab(zo, yo, p):
        ro = 2 * zo + yo
        return Pb.at[ro // RC, pl.ds(pl.multiple_of((ro % RC) * dr + p * dp, dp), dp)]

    def proto_z(zd, p):
        return send(my_cols(zd, p), slab(z, y, p), zs.at[zd, p], zr.at[z, p], (2 * zd + y, c))

    def proto_z_in(zo, p):
        return send(slab(zo, y, p), slab(zo, y, p), zs.at[zo, p], zr.at[zo, p], partner)

    def proto_y(zo, p, src=None):
        return send(slab(zo, y, p) if src is None else src, slab(zo, y, p), ys.at[zo, p], yr.at[zo, p], y_near)

    def proto_y_in(zo, p):
        return send(slab(zo, 1 - y, p), slab(zo, 1 - y, p), ys.at[zo, p], yr.at[zo, p], y_near)

    own = pltpu.make_async_copy(feat, G.at[z, c], lsem.at[0])
    mine = pltpu.make_async_copy(
        protos.at[:, pl.ds(pl.multiple_of(z * kl, kl), kl)],
        Pb.at[r // RC, pl.ds(pl.multiple_of((r % RC) * dr, dr), dr)],
        lsem.at[1],
    )
    own.start()
    mine.start()
    pl.semaphore_wait(barrier, 2 * Z + 1)

    for h in range(H):
        src = feat.at[pl.ds(h * hp, hp)]
        near(z, h, src).start()
        pair(0, z, h, src).start()
    order = [("line", h) for h in range(AHEAD)]
    for p in range(NP):
        order += [("proto", p)] + ([("line", AHEAD + p)] if AHEAD + p < H else [])
    order += [("line", h) for h in range(AHEAD + NP, H)]

    for kind, n in order:
        if kind == "proto":
            for k in range(Z - 1, 0, -1):
                sides(k, lambda o, side: proto_z(o, n).start())
            proto_y(z, n, my_cols(z, n)).start()
        else:
            src = feat.at[pl.ds(n * hp, hp)]

            @pl.when(z + 1 < Z)
            def _():
                line_up(z, n, src).start()

            @pl.when(z >= 1)
            def _():
                line_down(z, n, src).start()

    def do_line(k, h):
        def step(o, side):
            line_in(o, h).wait_recv()
            spread(o, side, h)

        sides(k, step)

    def do_near(k, h):
        def step(o, side):
            near_in(o, h).wait_recv()
            pair(1, o, h).start()

        sides(k, step)

    def do_proto(k, p):
        def step(o, side):
            proto_z_in(o, p).wait_recv()
            proto_y(o, p).start()

        sides(k, step)

    def turn(n, _):
        i, t = n // (kl // 256), n % (kl // 256)
        cols = pl.ds(pl.multiple_of(t * 256, 256), 256)
        PT[i, cols] = Pb[i, :, cols].astype(F32).T.astype(BF16)
        return 0

    def prepare():
        for p in range(NP):
            for zo in range(Z):
                proto_y_in(zo, p).wait_recv()
        mine.wait()
        lax.fori_loop(0, C * (kl // 256), turn, 0)
        own.wait()

    def fetch(o, cc, slot):
        if resident:
            return G.at[o, cc]
        load = pltpu.make_async_copy(G.at[o, cc], fbuf.at[slot], lsem.at[2 + slot])
        load.start()
        load.wait()
        return fbuf.at[slot]

    def lanes(j):
        return slice(j * LANES, (j + 1) * LANES)

    def fold(v):
        return jnp.sum(v.reshape(v.shape[0] // 8, 8, LANES), axis=0)

    def tile_rows(i):
        return pl.ds(pl.multiple_of(i * TILE, TILE), TILE)

    HT = H * 256 // Bl

    def unit(k, n):
        def step(o):
            for i in range(HT):
                for side in (0, 1):
                    pair_in(side, o, n * HT + i).wait_recv()
            rows = pl.ds(pl.multiple_of(n * 256, 256), 256)
            total = None
            for i in range(C):
                part = lax.dot_general(PT[i], fetch(o, i, i % 2)[rows], (((1,), (1,)), ((), ())), preferred_element_type=F32)
                total = part if total is None else total + part
            S[o, :, rows] = total
            js = tuple(pl.ds(pl.multiple_of(n * 256 + b * LANES, LANES), LANES) for b in (0, 1))

            def peak(i, m):
                part = pl.ds(pl.multiple_of(i * WIDE, WIDE), WIDE)
                return tuple(jnp.maximum(m[b], jnp.max(S[o, part, j].reshape(WIDE // 8, 8, LANES), axis=0)) for b, j in enumerate(js))

            floor = jnp.full((8, LANES), -jnp.inf, F32)
            tops = lax.fori_loop(0, kl // WIDE, peak, (floor,) * 2)
            tops = [jnp.max(t, axis=0, keepdims=True) for t in tops]

            def expo(i, acc):
                part = pl.ds(pl.multiple_of(i * WIDE, WIDE), WIDE)
                res = []
                for b, j in enumerate(js):
                    sh = S[o, part, j] - tops[b]
                    e2 = jnp.exp2(sh * K2)
                    e3 = jnp.exp2(sh * K3)
                    E[o, part, j] = e2
                    S[o, part, j] = e3
                    res.append((acc[b][0] + fold(e2), acc[b][1] + fold(e3)))
                return tuple(res)

            none = jnp.zeros((8, LANES), F32)
            sums = lax.fori_loop(0, kl // WIDE, expo, ((none, none),) * 2)
            for b, j in enumerate(js):
                st0[o, 0, :, j] = tops[b]
                st0[o, 1, :, j] = jnp.sum(sums[b][0], axis=0, keepdims=True)
                st0[o, 2, :, j] = jnp.sum(sums[b][1], axis=0, keepdims=True)

        def side(i, _):
            o = z + k * (2 * i - 1)

            @pl.when(jnp.logical_and(jnp.logical_and(o >= 0, o < Z), k + 1 - i > 0))
            def _():
                step(o)

            return 0

        lax.fori_loop(0, 2, side, 0)

    left = NP
    for kind, n in order:
        if kind == "line":
            do_line(1, n)
            continue
        for k in range(1, Z):
            do_proto(k, n)
        left -= 1
        if left == NP // 2:
            for h in range(H):
                do_near(0, h)
    for h in range(H - LAG):
        do_near(1, h)

    U = Bl // 256
    END = (Z - 1) * H
    FIRST = H + READY + 1
    while any((u - U + 1) * HT - 1 > u + FIRST - LAG for u in range(Z * U)):
        FIRST += 1

    def advance(i, _):
        @pl.when(i < END)
        def _():
            do_line(1 + i // H, i % H)

        back = i - LAG

        @pl.when(back < END)
        def _():
            do_near(1 + back // H, back % H)

        @pl.when(i == H + READY)
        def _():
            prepare()

        job = i - FIRST

        @pl.when(job >= 0)
        def _():
            unit(job // U, job % U)

        return 0

    lax.fori_loop(H, FIRST + Z * U, advance, 0)

    def half(g):
        return pl.ds(g * Zh, Zh)

    def cross_a(e, st, ra):
        return send(st.at[half(1 - core)], ra, xas.at[e], xar.at[e], partner)

    def cross_b(e, i, qs, q):
        return send(qs, q.at[me], xbs.at[e, i], xbr.at[e, i], plane(flip(i)))

    def cross_c(e, res, g):
        return send(res.at[half(g)], res.at[half(g)], xcs.at[e], xcr.at[e], partner)

    def meet(e, st, ra, qs, q, res, join):
        cross_a(e, st, ra).wait_recv()
        qs[...] = join([st[half(core)], ra[...]])
        for i in range(2 * Z - 1, 0, -1):
            cross_b(e, i, qs, q).start()
        q[me] = qs[...]
        for i in range(2 * Z - 1, 0, -1):
            cross_b(e, i, qs, q).wait_recv()
        res[half(core)] = join([q[i] for i in range(2 * Z)])
        cross_c(e, res, core).start()

    def join_stats(parts):
        top = functools.reduce(jnp.maximum, [p[:, 0] for p in parts])
        s2 = sum(p[:, 1] * jnp.exp2((p[:, 0] - top) * K2) for p in parts)
        s3 = sum(p[:, 2] * jnp.exp2((p[:, 0] - top) * K3) for p in parts)
        return jnp.stack([top, s2, s3], axis=1)

    def join_sum(parts):
        return functools.reduce(jnp.add, parts)

    def col(g, more):
        def tile(i, _):
            rows = tile_rows(i)
            acc = CA[rows] if more else None
            for o in range(Zh):
                for j in range(NJ):
                    m = E[g * Zh + o, rows, lanes(j)] * wv[g * Zh + o, :, lanes(j)]
                    acc = m if acc is None else acc + m
            CA[rows] = acc
            return 0

        lax.fori_loop(0, kl // TILE, tile, 0)

    def row(sweep, g):
        for n in range(Zh):
            o = g * Zh + n

            def tile(i, acc):
                rows = tile_rows(i)
                scale = cs[rows]
                return tuple(acc[j] + fold(E[o, rows, lanes(j)] * scale) for j in range(NJ))

            sums = lax.fori_loop(0, kl // TILE, tile, (jnp.zeros((8, LANES), F32),) * NJ)
            for j in range(NJ):
                st1[sweep, o, 0, :, lanes(j)] = jnp.sum(sums[j], axis=0, keepdims=True) * fv[o, :, lanes(j)]

    def scales(g):
        for n in range(Zh):
            o = g * Zh + n
            down = st0[o, 0] - res0[o, 0]
            f2 = jnp.exp2(down * K2)
            fv[o] = f2
            wv[o] = f2 / res0[o, 1]
            av[o] = jnp.exp2(down * K3) / (res0[o, 2] * loss_temp)

    def rescale(sweep, g):
        for n in range(Zh):
            o = g * Zh + n
            wv[o] = fv[o] / res1[sweep, o, 0]

    cross_a(0, st0, ra0).start()
    meet(0, st0, ra0, qs0, q0, res0, join_stats)
    scales(core)

    for sweep in range(ITERS):
        col(core, False)
        if sweep == 0:
            cross_c(0, res0, 1 - core).wait_recv()
            scales(1 - core)
        else:
            cross_c(sweep, res1.at[sweep - 1], 1 - core).wait_recv()
            rescale(sweep - 1, 1 - core)
        col(1 - core, True)
        kst[sweep] = jnp.sum(CA[...].T, axis=0, keepdims=True)
        swap = send(kst.at[sweep], krc.at[sweep], ks.at[sweep], kr.at[sweep], y_near)
        swap.start()
        swap.wait_recv()
        scale = ratio / (kst[sweep] + krc[sweep])
        cs[...] = jnp.broadcast_to(scale, (LANES, kl)).T
        row(sweep, 1 - core)
        args = [a.at[sweep] for a in (st1, ra1, qs1, q1, res1)]
        cross_a(sweep + 1, args[0], args[1]).start()
        row(sweep, core)
        meet(sweep + 1, *args, join_sum)
        rescale(sweep, core)

    cross_c(ITERS, res1.at[ITERS - 1], 1 - core).wait_recv()
    rescale(ITERS - 1, 1 - core)

    SPAN = min(TILE, kq)

    def span(i):
        return pl.ds(pl.multiple_of(i * SPAN, SPAN), SPAN)

    def slope(q):
        def tile(n, _):
            o, i = n // (kq // SPAN), n % (kq // SPAN)
            rows = span(q * (kq // SPAN) + i)
            scale = cs[rows] * (1.0 / loss_temp)
            for j in range(NJ):
                value = S[o, rows, lanes(j)] * av[o, :, lanes(j)] - E[o, rows, lanes(j)] * wv[o, :, lanes(j)] * scale
                SL[o, span(i), lanes(j)] = value.astype(BF16)
            return 0

        lax.fori_loop(0, Z * (kq // SPAN), tile, 0)

    own_chunk = 2 * z // RC
    low = jnp.where(z < Zh, 1, 0)

    def chunk(t):
        down = C - 1 - t
        down = jnp.where(down > own_chunk, down, down - 1)
        up = jnp.where(t < own_chunk, t, t + 1)
        return jnp.where(t == C - 1, own_chunk, low * down + (1 - low) * up)

    ds = dr // PARTS

    def block_rows(ro, s):
        return pl.ds(pl.multiple_of((ro % RC) * dr + s * ds, ds), ds)

    def piece_of(q, zo, s):
        return RY.at[q, zo, pl.ds(s * ds, ds)]

    def grad_y(q, zo, s):
        ro = 2 * zo + 1 - y
        return send(T.at[q, ro // RC, block_rows(ro, s)], piece_of(q, zo, s), gys.at[q, zo, s], gyr.at[q, zo, s], y_near)

    def out_part(zo, q, s):
        return out.at[pl.ds(s * ds, ds), pl.ds(pl.multiple_of(zo * kl + q * kq, kq), kq)]

    def grad_z(q, zo, s):
        return send(piece_of(q, zo, s), out_part(z, q, s), gzs.at[q, zo, s], gzr.at[q, z, s], (2 * zo + y, c))

    def grad_z_in(q, zo, s):
        return send(piece_of(q, zo, s), out_part(zo, q, s), gzs.at[q, zo, s], gzr.at[q, zo, s], partner)

    def keep(q, s):
        return pltpu.make_async_copy(piece_of(q, z, s), out_part(z, q, s), gzs.at[q, z, s])

    def grads(q, t):
        cc = chunk(t)
        total = None
        for o in range(Z):
            part = jnp.dot(SL[o], fetch(o, cc, o % 2)[...], preferred_element_type=F32)
            total = part if total is None else total + part
        T[q, cc] = total.T.astype(BF16)
        for n in range(RC // 2):
            for s in range(PARTS):
                grad_y(q, cc * (RC // 2) + n, s).start()

    def pass_on(q, t):
        cc = chunk(t)
        for n in range(RC // 2):
            zo = cc * (RC // 2) + n
            ro = 2 * zo + y
            for s in range(PARTS):
                grad_y(q, zo, s).wait_recv()
                part = pl.ds(s * ds, ds)
                RY[q, zo, part] = (T[q, cc, block_rows(ro, s)].astype(F32) + RY[q, zo, part].astype(F32)).astype(BF16)

                @pl.when(zo != z)
                def _():
                    grad_z(q, zo, s).start()

                @pl.when(zo == z)
                def _():
                    keep(q, s).start()

    def task(n, _):
        q, t = n // C, n % C

        @pl.when(t == 0)
        def _():
            slope(q)

        grads(q, t)

        @pl.when(q >= 1)
        def _():
            pass_on(q - 1, t)

        return 0

    def last(t, _):
        pass_on(NQ - 1, t)
        return 0

    lax.fori_loop(0, NQ * C, task, 0)
    lax.fori_loop(0, C, last, 0)

    def drain(o, _):
        for h in range(H):

            @pl.when(jnp.logical_and(o <= z, z + 1 < Z))
            def _():
                line_up(o, h).wait_send()

            @pl.when(jnp.logical_and(o >= z, z >= 1))
            def _():
                line_down(o, h).wait_send()

            near(o, h).wait_send()
            pair(0, o, h).wait_send()
            pair(1, o, h).wait_send()
        for p in range(NP):
            proto_y(o, p).wait_send()

            @pl.when(o != z)
            def _():
                proto_z(o, p).wait_send()

        return 0

    lax.fori_loop(0, Z, drain, 0)

    cross_a(0, st0, ra0).wait_send()
    cross_c(0, res0, core).wait_send()
    for i in range(1, 2 * Z):
        cross_b(0, i, qs0, q0).wait_send()
    for sweep in range(ITERS):
        args = [a.at[sweep] for a in (st1, ra1, qs1, q1, res1)]
        send(kst.at[sweep], krc.at[sweep], ks.at[sweep], kr.at[sweep], y_near).wait_send()
        cross_a(sweep + 1, args[0], args[1]).wait_send()
        cross_c(sweep + 1, args[4], core).wait_send()
        for i in range(1, 2 * Z):
            cross_b(sweep + 1, i, args[2], args[3]).wait_send()

    def finish(n, _):
        q, zo = n // Z, n % Z
        for s in range(PARTS):
            grad_y(q, zo, s).wait_send()

            @pl.when(zo != z)
            def _():
                grad_z(q, zo, s).wait_send()
                grad_z_in(q, zo, s).wait_recv()

            @pl.when(zo == z)
            def _():
                keep(q, s).wait()

        return 0

    lax.fori_loop(0, NQ * Z, finish, 0)


def solution(mesh):
    R, C = mesh.shape["rows"], mesh.shape["cls"]
    assert C == 4 and R % 8 == 0

    def local(features, prototypes):
        Bl, dl = features.shape
        dr, kc = prototypes.shape
        Z, RC = R // 2, R // C
        Zh = Z // 2
        kl = kc // Z
        kq = max(LANES, kl // 4)
        NQ = kl // kq
        NP = max(1, dr // 64)
        H = Bl // (128 if Z <= 4 else 256)
        X = ITERS + 1
        dma = pltpu.SemaphoreType.DMA
        V = pltpu.VMEM
        resident = Z * C * Bl * dl * 2 <= 13 * 1024 * 1024
        gather = (V((Z, C, Bl, dl), BF16),) if resident else (V((2, Bl, dl), BF16),)
        outs = (jax.ShapeDtypeStruct((dr, kc), BF16),)
        if not resident:
            outs += (jax.ShapeDtypeStruct((Z, C, Bl, dl), BF16),)
        res = pl.pallas_call(
            functools.partial(kernel, R, C, resident),
            out_shape=outs,
            in_specs=[pl.BlockSpec(memory_space=pl.ANY)] * 2,
            out_specs=(pl.BlockSpec(memory_space=pl.ANY),) * len(outs),
            scratch_shapes=[
                *gather,
                V((C, dl, kl), BF16),
                V((C, kl, dl), BF16),
                V((Z, kl, Bl), F32),
                V((Z, kl, Bl), F32),
                V((Z, kq, Bl), BF16),
                V((NQ, C, dl, kq), BF16),
                V((NQ, Z, dr, kq), BF16),
                V((kl, LANES), F32),
                V((kl, LANES), F32),
                V((ITERS, 1, kl), F32),
                V((ITERS, 1, kl), F32),
                V((Z, 3, 1, Bl), F32),
                V((Zh, 3, 1, Bl), F32),
                V((Zh, 3, 1, Bl), F32),
                V((2 * Z, Zh, 3, 1, Bl), F32),
                V((Z, 3, 1, Bl), F32),
                V((ITERS, Z, 1, 1, Bl), F32),
                V((ITERS, Zh, 1, 1, Bl), F32),
                V((ITERS, Zh, 1, 1, Bl), F32),
                V((ITERS, 2 * Z, Zh, 1, 1, Bl), F32),
                V((ITERS, Z, 1, 1, Bl), F32),
                V((Z, 1, Bl), F32),
                V((Z, 1, Bl), F32),
                V((Z, 1, Bl), F32),
                dma((4,)),
                dma((Z, H)),
                dma((Z, H)),
                dma((Z, H)),
                dma((Z, H)),
                dma((Z, H)),
                dma((2, Z, H)),
                dma((2, Z, H)),
                dma((Z, NP)),
                dma((Z, NP)),
                dma((Z, NP)),
                dma((Z, NP)),
                dma((X,)),
                dma((X,)),
                dma((X, 2 * Z)),
                dma((X, 2 * Z)),
                dma((X,)),
                dma((X,)),
                dma((ITERS,)),
                dma((ITERS,)),
                dma((NQ, Z, PARTS)),
                dma((NQ, Z, PARTS)),
                dma((NQ, Z, PARTS)),
                dma((NQ, Z, PARTS)),
            ],
            compiler_params=pltpu.CompilerParams(
                collective_id=0, has_side_effects=True, vmem_limit_bytes=62 * 1024 * 1024
            ),
        )(features, prototypes)
        return res[0].astype(F32)

    return jax.shard_map(
        local,
        mesh=mesh,
        in_specs=(P("rows", "cls"), P("rows", "cls")),
        out_specs=P("rows", "cls"),
        check_vma=False,
    )
```

```python
import functools
import math

import jax
import jax.numpy as jnp
from jax import lax
from jax.experimental import pallas as pl
from jax.experimental.pallas import tpu as pltpu
from jax.sharding import PartitionSpec as P

ITERS = 3
code_temp = 0.2
loss_temp = 0.3
K2 = math.log2(math.e) / code_temp
K3 = math.log2(math.e) / loss_temp

MESH = pl.DeviceIdType.MESH
F32 = jnp.float32
BF16 = jnp.bfloat16
PARTS = 2
LANES = 128
TILE = 256
WIDE = 256
LAG = 3
AHEAD = 3
READY = 2


def kernel(
    R, C, resident, feat, protos, out, *refs,
):
    if resident:
        G, fbuf = refs[0], None
        refs = refs[1:]
    else:
        G, fbuf = refs[:2]
        refs = refs[2:]
    (
        Pb, PT, S, E, SL, T, RY, CA, cs, kst, krc,
        st0, ra0, qs0, q0, res0, st1, ra1, qs1, q1, res1, wv, av, fv,
        lsem, up_s, dn_s, ln_r, ns, nr, ps, pr, zs, zr, ys, yr,
        xas, xar, xbs, xbr, xcs, xcr, ks, kr, gys, gyr, gzs, gzr,
    ) = refs
    Z = R // 2
    Zh = Z // 2
    RC = R // C
    Bl, dl = feat.shape
    H = ln_r.shape[1]
    hp = Bl // H
    dr, kc = protos.shape
    kl = kc // Z
    NQ, kq = T.shape[0], T.shape[3]
    NJ = Bl // LANES
    ratio = float(Bl * R) / float(kc * C)

    r = lax.axis_index("rows")
    c = lax.axis_index("cls")
    x, core = c // 2, c % 2
    z, y = r // 2, r % 2
    me = 2 * z + x
    x_near = (r, (1 - x) * 2 + core)
    y_near = (2 * z + 1 - y, c)
    partner = (r, x * 2 + 1 - core)

    def plane(t):
        return (2 * (t // 2) + y, 2 * (t % 2) + core)

    def flip(i):
        t, b = me, 1
        while b <= i:
            if (i // b) % 2:
                t = t + b * (1 - 2 * ((me // b) % 2))
            b *= 2
        return t

    barrier = pltpu.get_barrier_semaphore()
    for i in range(1, 2 * Z):
        pl.semaphore_signal(barrier, inc=1, device_id=plane(flip(i)), device_id_type=MESH)
    pl.semaphore_signal(barrier, inc=1, device_id=partner, device_id_type=MESH)
    pl.semaphore_signal(barrier, inc=1, device_id=y_near, device_id_type=MESH)

    def send(src, dst, send_sem, recv_sem, dest):
        return pltpu.make_async_remote_copy(
            src_ref=src, dst_ref=dst, send_sem=send_sem, recv_sem=recv_sem, device_id=dest, device_id_type=MESH
        )

    def piece(o, xx, co, h):
        return G.at[o, 2 * xx + co, pl.ds(h * hp, hp)]

    def origin(o, h, src):
        return piece(o, x, core, h) if src is None else src

    def line_up(o, h, src=None):
        return send(origin(o, h, src), piece(o, x, core, h), up_s.at[o, h], ln_r.at[o, h], (r + 2, c))

    def line_down(o, h, src=None):
        return send(origin(o, h, src), piece(o, x, core, h), dn_s.at[o, h], ln_r.at[o, h], (r - 2, c))

    def line_in(o, h):
        return send(piece(o, x, core, h), piece(o, x, core, h), up_s.at[o, h], ln_r.at[o, h], partner)

    def near(o, h, src=None):
        return send(origin(o, h, src), piece(o, x, core, h), ns.at[o, h], nr.at[o, h], x_near)

    def near_in(o, h):
        return send(piece(o, 1 - x, core, h), piece(o, 1 - x, core, h), ns.at[o, h], nr.at[o, h], x_near)

    def pair(side, o, h, src=None):
        xx = 1 - x if side else x
        dst = piece(o, xx, core, h)
        return send(dst if src is None else src, dst, ps.at[side, o, h], pr.at[side, o, h], partner)

    def pair_in(side, o, h):
        xx = 1 - x if side else x
        dst = piece(o, xx, 1 - core, h)
        return send(dst, dst, ps.at[side, o, h], pr.at[side, o, h], partner)

    def sides(k, fn):
        if isinstance(k, int) and k == 0:
            fn(z, 0)
            return

        @pl.when(z - k >= 0)
        def _():
            fn(z - k, -1)

        @pl.when(z + k < Z)
        def _():
            fn(z + k, 1)

    def spread(o, side, h, src=None):
        if side <= 0:

            @pl.when(z + 1 < Z)
            def _():
                line_up(o, h, src).start()

        if side >= 0:

            @pl.when(z >= 1)
            def _():
                line_down(o, h, src).start()

        near(o, h, src).start()
        pair(0, o, h, src).start()

    NP = max(1, dr // 64)
    dp = dr // NP

    def my_cols(zd, p):
        return protos.at[pl.ds(p * dp, dp), pl.ds(pl.multiple_of(zd * kl, kl), kl)]

    def slab(zo, yo, p):
        ro = 2 * zo + yo
        return Pb.at[ro // RC, pl.ds(pl.multiple_of((ro % RC) * dr + p * dp, dp), dp)]

    def proto_z(zd, p):
        return send(my_cols(zd, p), slab(z, y, p), zs.at[zd, p], zr.at[z, p], (2 * zd + y, c))

    def proto_z_in(zo, p):
        return send(slab(zo, y, p), slab(zo, y, p), zs.at[zo, p], zr.at[zo, p], partner)

    def proto_y(zo, p, src=None):
        return send(slab(zo, y, p) if src is None else src, slab(zo, y, p), ys.at[zo, p], yr.at[zo, p], y_near)

    def proto_y_in(zo, p):
        return send(slab(zo, 1 - y, p), slab(zo, 1 - y, p), ys.at[zo, p], yr.at[zo, p], y_near)

    own = pltpu.make_async_copy(feat, G.at[z, c], lsem.at[0])
    mine = pltpu.make_async_copy(
        protos.at[:, pl.ds(pl.multiple_of(z * kl, kl), kl)],
        Pb.at[r // RC, pl.ds(pl.multiple_of((r % RC) * dr, dr), dr)],
        lsem.at[1],
    )
    own.start()
    mine.start()
    pl.semaphore_wait(barrier, 2 * Z + 1)

    for h in range(H):
        src = feat.at[pl.ds(h * hp, hp)]
        near(z, h, src).start()
        pair(0, z, h, src).start()
    order = [("line", h) for h in range(AHEAD)]
    for p in range(NP):
        order += [("proto", p)] + ([("line", AHEAD + p)] if AHEAD + p < H else [])
    order += [("line", h) for h in range(AHEAD + NP, H)]

    for kind, n in order:
        if kind == "proto":
            for k in range(Z - 1, 0, -1):
                sides(k, lambda o, side: proto_z(o, n).start())
            proto_y(z, n, my_cols(z, n)).start()
        else:
            src = feat.at[pl.ds(n * hp, hp)]

            @pl.when(z + 1 < Z)
            def _():
                line_up(z, n, src).start()

            @pl.when(z >= 1)
            def _():
                line_down(z, n, src).start()

    def do_line(k, h):
        def step(o, side):
            line_in(o, h).wait_recv()
            spread(o, side, h)

        sides(k, step)

    def do_near(k, h):
        def step(o, side):
            near_in(o, h).wait_recv()
            pair(1, o, h).start()

        sides(k, step)

    def do_proto(k, p):
        def step(o, side):
            proto_z_in(o, p).wait_recv()
            proto_y(o, p).start()

        sides(k, step)

    def turn(n, _):
        i, t = n // (kl // 256), n % (kl // 256)
        cols = pl.ds(pl.multiple_of(t * 256, 256), 256)
        PT[i, cols] = Pb[i, :, cols].astype(F32).T.astype(BF16)
        return 0

    def prepare():
        for p in range(NP):
            for zo in range(Z):
                proto_y_in(zo, p).wait_recv()
        mine.wait()
        lax.fori_loop(0, C * (kl // 256), turn, 0)
        own.wait()

    def fetch(o, cc, slot):
        if resident:
            return G.at[o, cc]
        load = pltpu.make_async_copy(G.at[o, cc], fbuf.at[slot], lsem.at[2 + slot])
        load.start()
        load.wait()
        return fbuf.at[slot]

    def lanes(j):
        return slice(j * LANES, (j + 1) * LANES)

    def fold(v):
        return jnp.sum(v.reshape(v.shape[0] // 8, 8, LANES), axis=0)

    def tile_rows(i):
        return pl.ds(pl.multiple_of(i * TILE, TILE), TILE)

    HT = H * 256 // Bl

    def unit(k, n):
        def step(o):
            for i in range(HT):
                for side in (0, 1):
                    pair_in(side, o, n * HT + i).wait_recv()
            rows = pl.ds(pl.multiple_of(n * 256, 256), 256)
            total = None
            for i in range(C):
                part = lax.dot_general(PT[i], fetch(o, i, i % 2)[rows], (((1,), (1,)), ((), ())), preferred_element_type=F32)
                total = part if total is None else total + part
            S[o, :, rows] = total
            js = tuple(pl.ds(pl.multiple_of(n * 256 + b * LANES, LANES), LANES) for b in (0, 1))

            def peak(i, m):
                part = pl.ds(pl.multiple_of(i * WIDE, WIDE), WIDE)
                return tuple(jnp.maximum(m[b], jnp.max(S[o, part, j].reshape(WIDE // 8, 8, LANES), axis=0)) for b, j in enumerate(js))

            floor = jnp.full((8, LANES), -jnp.inf, F32)
            tops = lax.fori_loop(0, kl // WIDE, peak, (floor,) * 2)
            tops = [jnp.max(t, axis=0, keepdims=True) for t in tops]

            def expo(i, acc):
                part = pl.ds(pl.multiple_of(i * WIDE, WIDE), WIDE)
                res = []
                for b, j in enumerate(js):
                    sh = S[o, part, j] - tops[b]
                    e2 = jnp.exp2(sh * K2)
                    e3 = jnp.exp2(sh * K3)
                    E[o, part, j] = e2
                    S[o, part, j] = e3
                    res.append((acc[b][0] + fold(e2), acc[b][1] + fold(e3)))
                return tuple(res)

            none = jnp.zeros((8, LANES), F32)
            sums = lax.fori_loop(0, kl // WIDE, expo, ((none, none),) * 2)
            for b, j in enumerate(js):
                st0[o, 0, :, j] = tops[b]
                st0[o, 1, :, j] = jnp.sum(sums[b][0], axis=0, keepdims=True)
                st0[o, 2, :, j] = jnp.sum(sums[b][1], axis=0, keepdims=True)

        def side(i, _):
            o = z + k * (2 * i - 1)

            @pl.when(jnp.logical_and(jnp.logical_and(o >= 0, o < Z), k + 1 - i > 0))
            def _():
                step(o)

            return 0

        lax.fori_loop(0, 2, side, 0)

    left = NP
    for kind, n in order:
        if kind == "line":
            do_line(1, n)
            continue
        for k in range(1, Z):
            do_proto(k, n)
        left -= 1
        if left == NP // 2:
            for h in range(H):
                do_near(0, h)
    for h in range(H - LAG):
        do_near(1, h)

    U = Bl // 256
    END = (Z - 1) * H
    FIRST = H + READY + 1
    while any((u - U + 1) * HT - 1 > u + FIRST - LAG for u in range(Z * U)):
        FIRST += 1

    def advance(i, _):
        @pl.when(i < END)
        def _():
            do_line(1 + i // H, i % H)

        back = i - LAG

        @pl.when(back < END)
        def _():
            do_near(1 + back // H, back % H)

        @pl.when(i == H + READY)
        def _():
            prepare()

        job = i - FIRST

        @pl.when(job >= 0)
        def _():
            unit(job // U, job % U)

        return 0

    lax.fori_loop(H, FIRST + Z * U, advance, 0)

    def half(g):
        return pl.ds(g * Zh, Zh)

    def cross_a(e, st, ra):
        return send(st.at[half(1 - core)], ra, xas.at[e], xar.at[e], partner)

    def cross_b(e, i, qs, q):
        return send(qs, q.at[me], xbs.at[e, i], xbr.at[e, i], plane(flip(i)))

    def cross_c(e, res, g):
        return send(res.at[half(g)], res.at[half(g)], xcs.at[e], xcr.at[e], partner)

    def meet(e, st, ra, qs, q, res, join):
        cross_a(e, st, ra).wait_recv()
        qs[...] = join([st[half(core)], ra[...]])
        for i in range(2 * Z - 1, 0, -1):
            cross_b(e, i, qs, q).start()
        q[me] = qs[...]
        for i in range(2 * Z - 1, 0, -1):
            cross_b(e, i, qs, q).wait_recv()
        res[half(core)] = join([q[i] for i in range(2 * Z)])
        cross_c(e, res, core).start()

    def join_stats(parts):
        top = functools.reduce(jnp.maximum, [p[:, 0] for p in parts])
        s2 = sum(p[:, 1] * jnp.exp2((p[:, 0] - top) * K2) for p in parts)
        s3 = sum(p[:, 2] * jnp.exp2((p[:, 0] - top) * K3) for p in parts)
        return jnp.stack([top, s2, s3], axis=1)

    def join_sum(parts):
        return functools.reduce(jnp.add, parts)

    def col(g, more):
        def tile(i, _):
            rows = tile_rows(i)
            acc = CA[rows] if more else None
            for o in range(Zh):
                for j in range(NJ):
                    m = E[g * Zh + o, rows, lanes(j)] * wv[g * Zh + o, :, lanes(j)]
                    acc = m if acc is None else acc + m
            CA[rows] = acc
            return 0

        lax.fori_loop(0, kl // TILE, tile, 0)

    def row(sweep, g):
        for n in range(Zh):
            o = g * Zh + n

            def tile(i, acc):
                rows = tile_rows(i)
                scale = cs[rows]
                return tuple(acc[j] + fold(E[o, rows, lanes(j)] * scale) for j in range(NJ))

            sums = lax.fori_loop(0, kl // TILE, tile, (jnp.zeros((8, LANES), F32),) * NJ)
            for j in range(NJ):
                st1[sweep, o, 0, :, lanes(j)] = jnp.sum(sums[j], axis=0, keepdims=True) * fv[o, :, lanes(j)]

    def scales(g):
        for n in range(Zh):
            o = g * Zh + n
            down = st0[o, 0] - res0[o, 0]
            f2 = jnp.exp2(down * K2)
            fv[o] = f2
            wv[o] = f2 / res0[o, 1]
            av[o] = jnp.exp2(down * K3) / (res0[o, 2] * loss_temp)

    def rescale(sweep, g):
        for n in range(Zh):
            o = g * Zh + n
            wv[o] = fv[o] / res1[sweep, o, 0]

    cross_a(0, st0, ra0).start()
    meet(0, st0, ra0, qs0, q0, res0, join_stats)
    scales(core)

    for sweep in range(ITERS):
        col(core, False)
        if sweep == 0:
            cross_c(0, res0, 1 - core).wait_recv()
            scales(1 - core)
        else:
            cross_c(sweep, res1.at[sweep - 1], 1 - core).wait_recv()
            rescale(sweep - 1, 1 - core)
        col(1 - core, True)
        kst[sweep] = jnp.sum(CA[...].T, axis=0, keepdims=True)
        swap = send(kst.at[sweep], krc.at[sweep], ks.at[sweep], kr.at[sweep], y_near)
        swap.start()
        swap.wait_recv()
        scale = ratio / (kst[sweep] + krc[sweep])
        cs[...] = jnp.broadcast_to(scale, (LANES, kl)).T
        row(sweep, 1 - core)
        args = [a.at[sweep] for a in (st1, ra1, qs1, q1, res1)]
        cross_a(sweep + 1, args[0], args[1]).start()
        row(sweep, core)
        meet(sweep + 1, *args, join_sum)
        rescale(sweep, core)

    SPAN = min(TILE, kq)

    def span(i):
        return pl.ds(pl.multiple_of(i * SPAN, SPAN), SPAN)

    def slope(q, g):
        def tile(n, _):
            o, i = g * Zh + n // (kq // SPAN), n % (kq // SPAN)
            rows = span(q * (kq // SPAN) + i)
            scale = cs[rows] * (1.0 / loss_temp)
            for j in range(NJ):
                value = S[o, rows, lanes(j)] * av[o, :, lanes(j)] - E[o, rows, lanes(j)] * wv[o, :, lanes(j)] * scale
                SL[o, span(i), lanes(j)] = value.astype(BF16)
            return 0

        lax.fori_loop(0, Zh * (kq // SPAN), tile, 0)

    own_chunk = 2 * z // RC
    low = jnp.where(z < Zh, 1, 0)

    def chunk(t):
        down = C - 1 - t
        down = jnp.where(down > own_chunk, down, down - 1)
        up = jnp.where(t < own_chunk, t, t + 1)
        return jnp.where(t == C - 1, own_chunk, low * down + (1 - low) * up)

    ds = dr // PARTS

    def block_rows(ro, s):
        return pl.ds(pl.multiple_of((ro % RC) * dr + s * ds, ds), ds)

    def piece_of(q, zo, s):
        return RY.at[q, zo, pl.ds(s * ds, ds)]

    def grad_y(q, zo, s):
        ro = 2 * zo + 1 - y
        return send(T.at[q, ro // RC, block_rows(ro, s)], piece_of(q, zo, s), gys.at[q, zo, s], gyr.at[q, zo, s], y_near)

    def out_part(zo, q, s):
        return out.at[pl.ds(s * ds, ds), pl.ds(pl.multiple_of(zo * kl + q * kq, kq), kq)]

    def grad_z(q, zo, s):
        return send(piece_of(q, zo, s), out_part(z, q, s), gzs.at[q, zo, s], gzr.at[q, z, s], (2 * zo + y, c))

    def grad_z_in(q, zo, s):
        return send(piece_of(q, zo, s), out_part(zo, q, s), gzs.at[q, zo, s], gzr.at[q, zo, s], partner)

    def keep(q, s):
        return pltpu.make_async_copy(piece_of(q, z, s), out_part(z, q, s), gzs.at[q, z, s])

    def grads(q, t):
        cc = chunk(t)
        total = None
        for o in range(Z):
            part = jnp.dot(SL[o], fetch(o, cc, o % 2)[...], preferred_element_type=F32)
            total = part if total is None else total + part
        T[q, cc] = total.T.astype(BF16)
        for n in range(RC // 2):
            for s in range(PARTS):
                grad_y(q, cc * (RC // 2) + n, s).start()

    def pass_on(q, t):
        cc = chunk(t)
        for n in range(RC // 2):
            zo = cc * (RC // 2) + n
            ro = 2 * zo + y
            for s in range(PARTS):
                grad_y(q, zo, s).wait_recv()
                part = pl.ds(s * ds, ds)
                RY[q, zo, part] = (T[q, cc, block_rows(ro, s)].astype(F32) + RY[q, zo, part].astype(F32)).astype(BF16)

                @pl.when(zo != z)
                def _():
                    grad_z(q, zo, s).start()

                @pl.when(zo == z)
                def _():
                    keep(q, s).start()

    def task(n, _):
        q, t = n // C, n % C

        @pl.when(q >= 1)
        def _():
            pass_on(q - 1, t)

        @pl.when(jnp.logical_and(t == 0, q >= 1))
        def _():
            slope(q, core)
            slope(q, 1 - core)

        grads(q, t)
        return 0

    def last(t, _):
        pass_on(NQ - 1, t)
        return 0

    slope(0, core)
    cross_c(ITERS, res1.at[ITERS - 1], 1 - core).wait_recv()
    rescale(ITERS - 1, 1 - core)
    slope(0, 1 - core)
    lax.fori_loop(0, NQ * C, task, 0)
    lax.fori_loop(0, C, last, 0)

    def drain(o, _):
        for h in range(H):

            @pl.when(jnp.logical_and(o <= z, z + 1 < Z))
            def _():
                line_up(o, h).wait_send()

            @pl.when(jnp.logical_and(o >= z, z >= 1))
            def _():
                line_down(o, h).wait_send()

            near(o, h).wait_send()
            pair(0, o, h).wait_send()
            pair(1, o, h).wait_send()
        for p in range(NP):
            proto_y(o, p).wait_send()

            @pl.when(o != z)
            def _():
                proto_z(o, p).wait_send()

        return 0

    lax.fori_loop(0, Z, drain, 0)

    cross_a(0, st0, ra0).wait_send()
    cross_c(0, res0, core).wait_send()
    for i in range(1, 2 * Z):
        cross_b(0, i, qs0, q0).wait_send()
    for sweep in range(ITERS):
        args = [a.at[sweep] for a in (st1, ra1, qs1, q1, res1)]
        send(kst.at[sweep], krc.at[sweep], ks.at[sweep], kr.at[sweep], y_near).wait_send()
        cross_a(sweep + 1, args[0], args[1]).wait_send()
        cross_c(sweep + 1, args[4], core).wait_send()
        for i in range(1, 2 * Z):
            cross_b(sweep + 1, i, args[2], args[3]).wait_send()

    def finish(n, _):
        q, zo = n // Z, n % Z
        for s in range(PARTS):
            grad_y(q, zo, s).wait_send()

            @pl.when(zo != z)
            def _():
                grad_z(q, zo, s).wait_send()
                grad_z_in(q, zo, s).wait_recv()

            @pl.when(zo == z)
            def _():
                keep(q, s).wait()

        return 0

    lax.fori_loop(0, NQ * Z, finish, 0)


def solution(mesh):
    R, C = mesh.shape["rows"], mesh.shape["cls"]
    assert C == 4 and R % 8 == 0

    def local(features, prototypes):
        Bl, dl = features.shape
        dr, kc = prototypes.shape
        Z, RC = R // 2, R // C
        Zh = Z // 2
        kl = kc // Z
        kq = max(LANES, kl // 4)
        NQ = kl // kq
        NP = max(1, dr // 64)
        H = Bl // (128 if Z <= 4 else 256)
        X = ITERS + 1
        dma = pltpu.SemaphoreType.DMA
        V = pltpu.VMEM
        resident = Z * C * Bl * dl * 2 <= 13 * 1024 * 1024
        gather = (V((Z, C, Bl, dl), BF16),) if resident else (V((2, Bl, dl), BF16),)
        outs = (jax.ShapeDtypeStruct((dr, kc), BF16),)
        if not resident:
            outs += (jax.ShapeDtypeStruct((Z, C, Bl, dl), BF16),)
        res = pl.pallas_call(
            functools.partial(kernel, R, C, resident),
            out_shape=outs,
            in_specs=[pl.BlockSpec(memory_space=pl.ANY)] * 2,
            out_specs=(pl.BlockSpec(memory_space=pl.ANY),) * len(outs),
            scratch_shapes=[
                *gather,
                V((C, dl, kl), BF16),
                V((C, kl, dl), BF16),
                V((Z, kl, Bl), F32),
                V((Z, kl, Bl), F32),
                V((Z, kq, Bl), BF16),
                V((NQ, C, dl, kq), BF16),
                V((NQ, Z, dr, kq), BF16),
                V((kl, LANES), F32),
                V((kl, LANES), F32),
                V((ITERS, 1, kl), F32),
                V((ITERS, 1, kl), F32),
                V((Z, 3, 1, Bl), F32),
                V((Zh, 3, 1, Bl), F32),
                V((Zh, 3, 1, Bl), F32),
                V((2 * Z, Zh, 3, 1, Bl), F32),
                V((Z, 3, 1, Bl), F32),
                V((ITERS, Z, 1, 1, Bl), F32),
                V((ITERS, Zh, 1, 1, Bl), F32),
                V((ITERS, Zh, 1, 1, Bl), F32),
                V((ITERS, 2 * Z, Zh, 1, 1, Bl), F32),
                V((ITERS, Z, 1, 1, Bl), F32),
                V((Z, 1, Bl), F32),
                V((Z, 1, Bl), F32),
                V((Z, 1, Bl), F32),
                dma((4,)),
                dma((Z, H)),
                dma((Z, H)),
                dma((Z, H)),
                dma((Z, H)),
                dma((Z, H)),
                dma((2, Z, H)),
                dma((2, Z, H)),
                dma((Z, NP)),
                dma((Z, NP)),
                dma((Z, NP)),
                dma((Z, NP)),
                dma((X,)),
                dma((X,)),
                dma((X, 2 * Z)),
                dma((X, 2 * Z)),
                dma((X,)),
                dma((X,)),
                dma((ITERS,)),
                dma((ITERS,)),
                dma((NQ, Z, PARTS)),
                dma((NQ, Z, PARTS)),
                dma((NQ, Z, PARTS)),
                dma((NQ, Z, PARTS)),
            ],
            compiler_params=pltpu.CompilerParams(
                collective_id=0, has_side_effects=True, vmem_limit_bytes=62 * 1024 * 1024
            ),
        )(features, prototypes)
        return res[0].astype(F32)

    return jax.shard_map(
        local,
        mesh=mesh,
        in_specs=(P("rows", "cls"), P("rows", "cls")),
        out_specs=P("rows", "cls"),
        check_vma=False,
    )
```

```python
import functools
import math

import jax
import jax.numpy as jnp
from jax import lax
from jax.experimental import pallas as pl
from jax.experimental.pallas import tpu as pltpu
from jax.sharding import PartitionSpec as P

ITERS = 3
code_temp = 0.2
loss_temp = 0.3
K2 = math.log2(math.e) / code_temp
K3 = math.log2(math.e) / loss_temp

MESH = pl.DeviceIdType.MESH
F32 = jnp.float32
BF16 = jnp.bfloat16
PARTS = 2
LANES = 128
TILE = 256
WIDE = 512
LAG = 3
AHEAD = 3
READY = 2


def kernel(
    R, C, resident, feat, protos, out, *refs,
):
    if resident:
        G, fbuf = refs[0], None
        refs = refs[1:]
    else:
        G, fbuf = refs[:2]
        refs = refs[2:]
    (
        Pb, PT, S, E, SL, T, RY, CA, cs, kst, krc,
        st0, ra0, qs0, q0, res0, st1, ra1, qs1, q1, res1, wv, av, fv,
        lsem, up_s, dn_s, ln_r, ns, nr, ps, pr, zs, zr, ys, yr,
        xas, xar, xbs, xbr, xcs, xcr, ks, kr, gys, gyr, gzs, gzr,
    ) = refs
    Z = R // 2
    Zh = Z // 2
    RC = R // C
    Bl, dl = feat.shape
    H = ln_r.shape[1]
    hp = Bl // H
    dr, kc = protos.shape
    kl = kc // Z
    NQ, kq = T.shape[0], T.shape[3]
    NJ = Bl // LANES
    ratio = float(Bl * R) / float(kc * C)

    r = lax.axis_index("rows")
    c = lax.axis_index("cls")
    x, core = c // 2, c % 2
    z, y = r // 2, r % 2
    me = 2 * z + x
    x_near = (r, (1 - x) * 2 + core)
    y_near = (2 * z + 1 - y, c)
    partner = (r, x * 2 + 1 - core)

    def plane(t):
        return (2 * (t // 2) + y, 2 * (t % 2) + core)

    def flip(i):
        t, b = me, 1
        while b <= i:
            if (i // b) % 2:
                t = t + b * (1 - 2 * ((me // b) % 2))
            b *= 2
        return t

    barrier = pltpu.get_barrier_semaphore()
    for i in range(1, 2 * Z):
        pl.semaphore_signal(barrier, inc=1, device_id=plane(flip(i)), device_id_type=MESH)
    pl.semaphore_signal(barrier, inc=1, device_id=partner, device_id_type=MESH)
    pl.semaphore_signal(barrier, inc=1, device_id=y_near, device_id_type=MESH)

    def send(src, dst, send_sem, recv_sem, dest):
        return pltpu.make_async_remote_copy(
            src_ref=src, dst_ref=dst, send_sem=send_sem, recv_sem=recv_sem, device_id=dest, device_id_type=MESH
        )

    def piece(o, xx, co, h):
        return G.at[o, 2 * xx + co, pl.ds(h * hp, hp)]

    def origin(o, h, src):
        return piece(o, x, core, h) if src is None else src

    def line_up(o, h, src=None):
        return send(origin(o, h, src), piece(o, x, core, h), up_s.at[o, h], ln_r.at[o, h], (r + 2, c))

    def line_down(o, h, src=None):
        return send(origin(o, h, src), piece(o, x, core, h), dn_s.at[o, h], ln_r.at[o, h], (r - 2, c))

    def line_in(o, h):
        return send(piece(o, x, core, h), piece(o, x, core, h), up_s.at[o, h], ln_r.at[o, h], partner)

    def near(o, h, src=None):
        return send(origin(o, h, src), piece(o, x, core, h), ns.at[o, h], nr.at[o, h], x_near)

    def near_in(o, h):
        return send(piece(o, 1 - x, core, h), piece(o, 1 - x, core, h), ns.at[o, h], nr.at[o, h], x_near)

    def pair(side, o, h, src=None):
        xx = 1 - x if side else x
        dst = piece(o, xx, core, h)
        return send(dst if src is None else src, dst, ps.at[side, o, h], pr.at[side, o, h], partner)

    def pair_in(side, o, h):
        xx = 1 - x if side else x
        dst = piece(o, xx, 1 - core, h)
        return send(dst, dst, ps.at[side, o, h], pr.at[side, o, h], partner)

    def sides(k, fn):
        if isinstance(k, int) and k == 0:
            fn(z, 0)
            return

        @pl.when(z - k >= 0)
        def _():
            fn(z - k, -1)

        @pl.when(z + k < Z)
        def _():
            fn(z + k, 1)

    def spread(o, side, h, src=None):
        if side <= 0:

            @pl.when(z + 1 < Z)
            def _():
                line_up(o, h, src).start()

        if side >= 0:

            @pl.when(z >= 1)
            def _():
                line_down(o, h, src).start()

        near(o, h, src).start()
        pair(0, o, h, src).start()

    NP = max(1, dr // 64)
    dp = dr // NP

    def my_cols(zd, p):
        return protos.at[pl.ds(p * dp, dp), pl.ds(pl.multiple_of(zd * kl, kl), kl)]

    def slab(zo, yo, p):
        ro = 2 * zo + yo
        return Pb.at[ro // RC, pl.ds(pl.multiple_of((ro % RC) * dr + p * dp, dp), dp)]

    def proto_z(zd, p):
        return send(my_cols(zd, p), slab(z, y, p), zs.at[zd, p], zr.at[z, p], (2 * zd + y, c))

    def proto_z_in(zo, p):
        return send(slab(zo, y, p), slab(zo, y, p), zs.at[zo, p], zr.at[zo, p], partner)

    def proto_y(zo, p, src=None):
        return send(slab(zo, y, p) if src is None else src, slab(zo, y, p), ys.at[zo, p], yr.at[zo, p], y_near)

    def proto_y_in(zo, p):
        return send(slab(zo, 1 - y, p), slab(zo, 1 - y, p), ys.at[zo, p], yr.at[zo, p], y_near)

    own = pltpu.make_async_copy(feat, G.at[z, c], lsem.at[0])
    mine = pltpu.make_async_copy(
        protos.at[:, pl.ds(pl.multiple_of(z * kl, kl), kl)],
        Pb.at[r // RC, pl.ds(pl.multiple_of((r % RC) * dr, dr), dr)],
        lsem.at[1],
    )
    own.start()
    mine.start()
    pl.semaphore_wait(barrier, 2 * Z + 1)

    for h in range(H):
        src = feat.at[pl.ds(h * hp, hp)]
        near(z, h, src).start()
        pair(0, z, h, src).start()
    order = [("line", h) for h in range(AHEAD)]
    for p in range(NP):
        order += [("proto", p)] + ([("line", AHEAD + p)] if AHEAD + p < H else [])
    order += [("line", h) for h in range(AHEAD + NP, H)]

    for kind, n in order:
        if kind == "proto":
            for k in range(Z - 1, 0, -1):
                sides(k, lambda o, side: proto_z(o, n).start())
            proto_y(z, n, my_cols(z, n)).start()
        else:
            src = feat.at[pl.ds(n * hp, hp)]

            @pl.when(z + 1 < Z)
            def _():
                line_up(z, n, src).start()

            @pl.when(z >= 1)
            def _():
                line_down(z, n, src).start()

    def do_line(k, h):
        def step(o, side):
            line_in(o, h).wait_recv()
            spread(o, side, h)

        sides(k, step)

    def do_near(k, h):
        def step(o, side):
            near_in(o, h).wait_recv()
            pair(1, o, h).start()

        sides(k, step)

    def do_proto(k, p):
        def step(o, side):
            proto_z_in(o, p).wait_recv()
            proto_y(o, p).start()

        sides(k, step)

    def turn(n, _):
        i, t = n // (kl // 256), n % (kl // 256)
        cols = pl.ds(pl.multiple_of(t * 256, 256), 256)
        PT[i, cols] = Pb[i, :, cols].astype(F32).T.astype(BF16)
        return 0

    def prepare():
        for p in range(NP):
            for zo in range(Z):
                proto_y_in(zo, p).wait_recv()
        mine.wait()
        lax.fori_loop(0, C * (kl // 256), turn, 0)
        own.wait()

    def fetch(o, cc, slot):
        if resident:
            return G.at[o, cc]
        load = pltpu.make_async_copy(G.at[o, cc], fbuf.at[slot], lsem.at[2 + slot])
        load.start()
        load.wait()
        return fbuf.at[slot]

    def lanes(j):
        return slice(j * LANES, (j + 1) * LANES)

    def fold(v):
        return jnp.sum(v.reshape(v.shape[0] // 8, 8, LANES), axis=0)

    def tile_rows(i):
        return pl.ds(pl.multiple_of(i * TILE, TILE), TILE)

    HT = H * 256 // Bl
    wide = min(WIDE, kl)

    def unit(k, n):
        def step(o):
            for i in range(HT):
                for side in (0, 1):
                    pair_in(side, o, n * HT + i).wait_recv()
            rows = pl.ds(pl.multiple_of(n * 256, 256), 256)
            total = None
            for i in range(C):
                part = lax.dot_general(PT[i], fetch(o, i, i % 2)[rows], (((1,), (1,)), ((), ())), preferred_element_type=F32)
                total = part if total is None else total + part
            S[o, :, rows] = total
            js = tuple(pl.ds(pl.multiple_of(n * 256 + b * LANES, LANES), LANES) for b in (0, 1))

            def peak(i, m):
                part = pl.ds(pl.multiple_of(i * wide, wide), wide)
                return tuple(jnp.maximum(m[b], jnp.max(S[o, part, j].reshape(wide // 8, 8, LANES), axis=0)) for b, j in enumerate(js))

            floor = jnp.full((8, LANES), -jnp.inf, F32)
            tops = lax.fori_loop(0, kl // wide, peak, (floor,) * 2)
            tops = [jnp.max(t, axis=0, keepdims=True) for t in tops]

            def expo(i, acc):
                part = pl.ds(pl.multiple_of(i * wide, wide), wide)
                res = []
                for b, j in enumerate(js):
                    sh = S[o, part, j] - tops[b]
                    e2 = jnp.exp2(sh * K2)
                    e3 = jnp.exp2(sh * K3)
                    E[o, part, j] = e2
                    S[o, part, j] = e3
                    res.append((acc[b][0] + fold(e2), acc[b][1] + fold(e3)))
                return tuple(res)

            none = jnp.zeros((8, LANES), F32)
            sums = lax.fori_loop(0, kl // wide, expo, ((none, none),) * 2)
            for b, j in enumerate(js):
                st0[o, 0, :, j] = tops[b]
                st0[o, 1, :, j] = jnp.sum(sums[b][0], axis=0, keepdims=True)
                st0[o, 2, :, j] = jnp.sum(sums[b][1], axis=0, keepdims=True)

        def side(i, _):
            o = z + k * (2 * i - 1)

            @pl.when(jnp.logical_and(jnp.logical_and(o >= 0, o < Z), k + 1 - i > 0))
            def _():
                step(o)

            return 0

        lax.fori_loop(0, 2, side, 0)

    left = NP
    for kind, n in order:
        if kind == "line":
            do_line(1, n)
            continue
        for k in range(1, Z):
            do_proto(k, n)
        left -= 1
        if left == NP // 2:
            for h in range(H):
                do_near(0, h)
    for h in range(H - LAG):
        do_near(1, h)

    U = Bl // 256
    END = (Z - 1) * H
    FIRST = H + READY + 1
    while any((u - U + 1) * HT - 1 > u + FIRST - LAG for u in range(Z * U)):
        FIRST += 1

    def advance(i, _):
        @pl.when(i < END)
        def _():
            do_line(1 + i // H, i % H)

        back = i - LAG

        @pl.when(back < END)
        def _():
            do_near(1 + back // H, back % H)

        @pl.when(i == H + READY)
        def _():
            prepare()

        job = i - FIRST

        @pl.when(job >= 0)
        def _():
            unit(job // U, job % U)

        return 0

    lax.fori_loop(H, FIRST + Z * U, advance, 0)

    def half(g):
        return pl.ds(g * Zh, Zh)

    def cross_a(e, st, ra):
        return send(st.at[half(1 - core)], ra, xas.at[e], xar.at[e], partner)

    def cross_b(e, i, qs, q):
        return send(qs, q.at[me], xbs.at[e, i], xbr.at[e, i], plane(flip(i)))

    def cross_c(e, res, g):
        return send(res.at[half(g)], res.at[half(g)], xcs.at[e], xcr.at[e], partner)

    def meet(e, st, ra, qs, q, res, join):
        cross_a(e, st, ra).wait_recv()
        qs[...] = join([st[half(core)], ra[...]])
        for i in range(2 * Z - 1, 0, -1):
            cross_b(e, i, qs, q).start()
        q[me] = qs[...]
        for i in range(2 * Z - 1, 0, -1):
            cross_b(e, i, qs, q).wait_recv()
        res[half(core)] = join([q[i] for i in range(2 * Z)])
        cross_c(e, res, core).start()

    def join_stats(parts):
        top = functools.reduce(jnp.maximum, [p[:, 0] for p in parts])
        s2 = sum(p[:, 1] * jnp.exp2((p[:, 0] - top) * K2) for p in parts)
        s3 = sum(p[:, 2] * jnp.exp2((p[:, 0] - top) * K3) for p in parts)
        return jnp.stack([top, s2, s3], axis=1)

    def join_sum(parts):
        return functools.reduce(jnp.add, parts)

    def col(g, more):
        def tile(i, _):
            rows = tile_rows(i)
            acc = CA[rows] if more else None
            for o in range(Zh):
                for j in range(NJ):
                    m = E[g * Zh + o, rows, lanes(j)] * wv[g * Zh + o, :, lanes(j)]
                    acc = m if acc is None else acc + m
            CA[rows] = acc
            return 0

        lax.fori_loop(0, kl // TILE, tile, 0)

    def row(sweep, g):
        for n in range(Zh):
            o = g * Zh + n

            def tile(i, acc):
                rows = tile_rows(i)
                scale = cs[rows]
                return tuple(acc[j] + fold(E[o, rows, lanes(j)] * scale) for j in range(NJ))

            sums = lax.fori_loop(0, kl // TILE, tile, (jnp.zeros((8, LANES), F32),) * NJ)
            for j in range(NJ):
                st1[sweep, o, 0, :, lanes(j)] = jnp.sum(sums[j], axis=0, keepdims=True) * fv[o, :, lanes(j)]

    def scales(g):
        for n in range(Zh):
            o = g * Zh + n
            down = st0[o, 0] - res0[o, 0]
            f2 = jnp.exp2(down * K2)
            fv[o] = f2
            wv[o] = f2 / res0[o, 1]
            av[o] = jnp.exp2(down * K3) / (res0[o, 2] * loss_temp)

    def rescale(sweep, g):
        for n in range(Zh):
            o = g * Zh + n
            wv[o] = fv[o] / res1[sweep, o, 0]

    cross_a(0, st0, ra0).start()
    meet(0, st0, ra0, qs0, q0, res0, join_stats)
    scales(core)

    for sweep in range(ITERS):
        col(core, False)
        if sweep == 0:
            cross_c(0, res0, 1 - core).wait_recv()
            scales(1 - core)
        else:
            cross_c(sweep, res1.at[sweep - 1], 1 - core).wait_recv()
            rescale(sweep - 1, 1 - core)
        col(1 - core, True)
        kst[sweep] = jnp.sum(CA[...].T, axis=0, keepdims=True)
        swap = send(kst.at[sweep], krc.at[sweep], ks.at[sweep], kr.at[sweep], y_near)
        swap.start()
        swap.wait_recv()
        scale = ratio / (kst[sweep] + krc[sweep])
        cs[...] = jnp.broadcast_to(scale, (LANES, kl)).T
        row(sweep, 1 - core)
        args = [a.at[sweep] for a in (st1, ra1, qs1, q1, res1)]
        cross_a(sweep + 1, args[0], args[1]).start()
        row(sweep, core)
        meet(sweep + 1, *args, join_sum)
        rescale(sweep, core)

    SPAN = min(TILE, kq)

    def span(i):
        return pl.ds(pl.multiple_of(i * SPAN, SPAN), SPAN)

    def slope(q, g):
        def tile(n, _):
            o, i = g * Zh + n // (kq // SPAN), n % (kq // SPAN)
            rows = span(q * (kq // SPAN) + i)
            scale = cs[rows] * (1.0 / loss_temp)
            for j in range(NJ):
                value = S[o, rows, lanes(j)] * av[o, :, lanes(j)] - E[o, rows, lanes(j)] * wv[o, :, lanes(j)] * scale
                SL[o, span(i), lanes(j)] = value.astype(BF16)
            return 0

        lax.fori_loop(0, Zh * (kq // SPAN), tile, 0)

    own_chunk = 2 * z // RC
    low = jnp.where(z < Zh, 1, 0)

    def chunk(t):
        down = C - 1 - t
        down = jnp.where(down > own_chunk, down, down - 1)
        up = jnp.where(t < own_chunk, t, t + 1)
        return jnp.where(t == C - 1, own_chunk, low * down + (1 - low) * up)

    ds = dr // PARTS

    def block_rows(ro, s):
        return pl.ds(pl.multiple_of((ro % RC) * dr + s * ds, ds), ds)

    def piece_of(q, zo, s):
        return RY.at[q, zo, pl.ds(s * ds, ds)]

    def grad_y(q, zo, s):
        ro = 2 * zo + 1 - y
        return send(T.at[q, ro // RC, block_rows(ro, s)], piece_of(q, zo, s), gys.at[q, zo, s], gyr.at[q, zo, s], y_near)

    def out_part(zo, q, s):
        return out.at[pl.ds(s * ds, ds), pl.ds(pl.multiple_of(zo * kl + q * kq, kq), kq)]

    def grad_z(q, zo, s):
        return send(piece_of(q, zo, s), out_part(z, q, s), gzs.at[q, zo, s], gzr.at[q, z, s], (2 * zo + y, c))

    def grad_z_in(q, zo, s):
        return send(piece_of(q, zo, s), out_part(zo, q, s), gzs.at[q, zo, s], gzr.at[q, zo, s], partner)

    def keep(q, s):
        return pltpu.make_async_copy(piece_of(q, z, s), out_part(z, q, s), gzs.at[q, z, s])

    def grads(q, t):
        cc = chunk(t)
        total = None
        for o in range(Z):
            part = jnp.dot(SL[o], fetch(o, cc, o % 2)[...], preferred_element_type=F32)
            total = part if total is None else total + part
        T[q, cc] = total.T.astype(BF16)
        for n in range(RC // 2):
            for s in range(PARTS):
                grad_y(q, cc * (RC // 2) + n, s).start()

    def pass_on(q, t):
        cc = chunk(t)
        for n in range(RC // 2):
            zo = cc * (RC // 2) + n
            ro = 2 * zo + y
            for s in range(PARTS):
                grad_y(q, zo, s).wait_recv()
                part = pl.ds(s * ds, ds)
                RY[q, zo, part] = (T[q, cc, block_rows(ro, s)].astype(F32) + RY[q, zo, part].astype(F32)).astype(BF16)

                @pl.when(zo != z)
                def _():
                    grad_z(q, zo, s).start()

                @pl.when(zo == z)
                def _():
                    keep(q, s).start()

    def task(n, _):
        q, t = n // C, n % C

        @pl.when(q >= 1)
        def _():
            pass_on(q - 1, t)

        @pl.when(jnp.logical_and(t == 0, q >= 1))
        def _():
            slope(q, core)
            slope(q, 1 - core)

        grads(q, t)
        return 0

    def last(t, _):
        pass_on(NQ - 1, t)
        return 0

    slope(0, core)
    cross_c(ITERS, res1.at[ITERS - 1], 1 - core).wait_recv()
    rescale(ITERS - 1, 1 - core)
    slope(0, 1 - core)
    lax.fori_loop(0, NQ * C, task, 0)
    lax.fori_loop(0, C, last, 0)

    def drain(o, _):
        for h in range(H):

            @pl.when(jnp.logical_and(o <= z, z + 1 < Z))
            def _():
                line_up(o, h).wait_send()

            @pl.when(jnp.logical_and(o >= z, z >= 1))
            def _():
                line_down(o, h).wait_send()

            near(o, h).wait_send()
            pair(0, o, h).wait_send()
            pair(1, o, h).wait_send()
        for p in range(NP):
            proto_y(o, p).wait_send()

            @pl.when(o != z)
            def _():
                proto_z(o, p).wait_send()

        return 0

    lax.fori_loop(0, Z, drain, 0)

    cross_a(0, st0, ra0).wait_send()
    cross_c(0, res0, core).wait_send()
    for i in range(1, 2 * Z):
        cross_b(0, i, qs0, q0).wait_send()
    for sweep in range(ITERS):
        args = [a.at[sweep] for a in (st1, ra1, qs1, q1, res1)]
        send(kst.at[sweep], krc.at[sweep], ks.at[sweep], kr.at[sweep], y_near).wait_send()
        cross_a(sweep + 1, args[0], args[1]).wait_send()
        cross_c(sweep + 1, args[4], core).wait_send()
        for i in range(1, 2 * Z):
            cross_b(sweep + 1, i, args[2], args[3]).wait_send()

    def finish(n, _):
        q, zo = n // Z, n % Z
        for s in range(PARTS):
            grad_y(q, zo, s).wait_send()

            @pl.when(zo != z)
            def _():
                grad_z(q, zo, s).wait_send()
                grad_z_in(q, zo, s).wait_recv()

            @pl.when(zo == z)
            def _():
                keep(q, s).wait()

        return 0

    lax.fori_loop(0, NQ * Z, finish, 0)


def solution(mesh):
    R, C = mesh.shape["rows"], mesh.shape["cls"]
    assert C == 4 and R % 8 == 0

    def local(features, prototypes):
        Bl, dl = features.shape
        dr, kc = prototypes.shape
        Z, RC = R // 2, R // C
        Zh = Z // 2
        kl = kc // Z
        kq = max(LANES, kl // 4)
        NQ = kl // kq
        NP = max(1, dr // 64)
        H = Bl // (128 if Z <= 4 else 256)
        X = ITERS + 1
        dma = pltpu.SemaphoreType.DMA
        V = pltpu.VMEM
        resident = Z * C * Bl * dl * 2 <= 13 * 1024 * 1024
        gather = (V((Z, C, Bl, dl), BF16),) if resident else (V((2, Bl, dl), BF16),)
        outs = (jax.ShapeDtypeStruct((dr, kc), BF16),)
        if not resident:
            outs += (jax.ShapeDtypeStruct((Z, C, Bl, dl), BF16),)
        res = pl.pallas_call(
            functools.partial(kernel, R, C, resident),
            out_shape=outs,
            in_specs=[pl.BlockSpec(memory_space=pl.ANY)] * 2,
            out_specs=(pl.BlockSpec(memory_space=pl.ANY),) * len(outs),
            scratch_shapes=[
                *gather,
                V((C, dl, kl), BF16),
                V((C, kl, dl), BF16),
                V((Z, kl, Bl), F32),
                V((Z, kl, Bl), F32),
                V((Z, kq, Bl), BF16),
                V((NQ, C, dl, kq), BF16),
                V((NQ, Z, dr, kq), BF16),
                V((kl, LANES), F32),
                V((kl, LANES), F32),
                V((ITERS, 1, kl), F32),
                V((ITERS, 1, kl), F32),
                V((Z, 3, 1, Bl), F32),
                V((Zh, 3, 1, Bl), F32),
                V((Zh, 3, 1, Bl), F32),
                V((2 * Z, Zh, 3, 1, Bl), F32),
                V((Z, 3, 1, Bl), F32),
                V((ITERS, Z, 1, 1, Bl), F32),
                V((ITERS, Zh, 1, 1, Bl), F32),
                V((ITERS, Zh, 1, 1, Bl), F32),
                V((ITERS, 2 * Z, Zh, 1, 1, Bl), F32),
                V((ITERS, Z, 1, 1, Bl), F32),
                V((Z, 1, Bl), F32),
                V((Z, 1, Bl), F32),
                V((Z, 1, Bl), F32),
                dma((4,)),
                dma((Z, H)),
                dma((Z, H)),
                dma((Z, H)),
                dma((Z, H)),
                dma((Z, H)),
                dma((2, Z, H)),
                dma((2, Z, H)),
                dma((Z, NP)),
                dma((Z, NP)),
                dma((Z, NP)),
                dma((Z, NP)),
                dma((X,)),
                dma((X,)),
                dma((X, 2 * Z)),
                dma((X, 2 * Z)),
                dma((X,)),
                dma((X,)),
                dma((ITERS,)),
                dma((ITERS,)),
                dma((NQ, Z, PARTS)),
                dma((NQ, Z, PARTS)),
                dma((NQ, Z, PARTS)),
                dma((NQ, Z, PARTS)),
            ],
            compiler_params=pltpu.CompilerParams(
                collective_id=0, has_side_effects=True, vmem_limit_bytes=62 * 1024 * 1024
            ),
        )(features, prototypes)
        return res[0].astype(F32)

    return jax.shard_map(
        local,
        mesh=mesh,
        in_specs=(P("rows", "cls"), P("rows", "cls")),
        out_specs=P("rows", "cls"),
        check_vma=False,
    )
```
